32 devices in a mesh: les: 8 (over y, x, core), modes: 4 (over z).
Axes of the slice: x: 2, y: 2, z: 4, core: 2. Of those that a mesh axis runs over, the one named last changes fastest.
Arguments:
- pressure: bfloat16 [65536, 512], P('les', 'modes'), may hold values from -6 to 6
- targets: int32 [65536], P('les'), may hold values from 0 to 32767, as said below
- counts: int32 [8], P('les'), may hold values from 1 to 8192, as said below
- pseudo_inverse: bfloat16 [2, 1536, 16384], P(None, None, ('les', 'modes')), may hold values from -0.046875 to 0.046875
Outputs:
- harmonics: float32 [2, 2, 8, 1536], P(None, None, None, ('les', 'modes'))
The draws below stay inside these ranges and needn't reach their ends.
Inputs may be any that keep to these rules, and one draw needn't show every extreme that they name: `counts`: some partition holds exactly 8192 live faces; all partitions together hold 32768. `targets`: the live slots (slot f of partition i with f < counts[i]) name every station point exactly once. Point p of a station lies in the point rows of les index p // (512 * 4); at most 1024 live faces of one partition lie in the point rows of one les index, and some partition reaches that bound. Slots that are not live hold arbitrary indices in the range.
All inputs are finite; a program needn't handle non-finite values.
Results may differ from the reference program's by a relative error of at most 0.0003.
Values may be sent and summed in bfloat16 or wider, within the bound.
A program may use at most 64 MiB of HBM per device.

```python
import math
import jax
import jax.numpy as jnp
from jax import lax

STATIONS = 2
MODES = 1536
TIME = 512
HARM = 8
PT_DEV = 512
POINTS = 16384
FACE_CAP = 8192
N_LES = 8
N_MODES = 4


def face_layout(key):
    rows_les = PT_DEV * N_MODES
    per_owner = STATIONS * rows_les
    key_busy, key_spread, key_shuffle, key_dead, key_order = jax.random.split(jax.random.fold_in(key, 11), 5)
    busiest = jax.random.randint(key_busy, (), 0, N_LES)
    spread = jax.random.randint(key_spread, (per_owner,), 0, N_LES - 1)
    spread = spread + (spread >= busiest).astype(jnp.int32)
    partition_ids = jnp.arange(N_LES, dtype=jnp.int32)
    removed = jnp.sum((spread[:, None] == partition_ids[None, :]).astype(jnp.int32), axis=0)
    counts = per_owner - removed + per_owner * (partition_ids == busiest).astype(jnp.int32)
    offsets = jnp.cumsum(counts) - counts
    slot_ids = jnp.arange(FACE_CAP, dtype=jnp.int32)
    face_ranks = offsets[:, None] + slot_ids[None, :]
    is_alive = slot_ids[None, :] < counts[:, None]
    owner_les = face_ranks % N_LES
    within = jnp.minimum(face_ranks // N_LES, per_owner - 1)
    shuffles = jax.vmap(lambda sub_key: jax.random.permutation(sub_key, per_owner))(jax.random.split(key_shuffle, N_LES))
    chosen = shuffles[owner_les, within]
    station_ids = chosen // rows_les
    point_ids = owner_les * rows_les + chosen % rows_les
    live_targets = (station_ids * POINTS + point_ids).astype(jnp.int32)
    slot_order = jax.vmap(lambda sub_key: jax.random.permutation(sub_key, FACE_CAP))(jax.random.split(key_order, N_LES))
    scores = jnp.where(is_alive, slot_order, slot_order + FACE_CAP).astype(jnp.int32)
    order = jnp.argsort(scores, axis=1, stable=True).astype(jnp.int32)
    shuffled = jnp.take_along_axis(live_targets, order, axis=1)
    dead_targets = jax.random.randint(key_dead, (N_LES, FACE_CAP), 0, STATIONS * POINTS)
    targets = jnp.where(is_alive, shuffled, dead_targets).reshape(N_LES * FACE_CAP)
    return (counts.astype(jnp.int32), targets.astype(jnp.int32))


def draw_counts(key, part):
    return face_layout(key)[0]


def draw_targets(key, part):
    return face_layout(key)[1]


def block_scale(key, extent, cuts, smallest, high):
    level = 1.0
    for axis_at, parts in cuts:
        steps = jax.random.uniform(jax.random.fold_in(jax.random.fold_in(key, 6), axis_at), (parts,), jnp.float32, smallest / len(cuts), high / len(cuts))
        level = level * jnp.repeat(jnp.exp(steps), extent[axis_at] // parts).reshape((-1,) + (1,) * (len(extent) - 1 - axis_at))
    return level


def bell_draw(stream_key, dims, width, limit, pieces=(), held_as=jnp.bfloat16):
    entries = jax.random.normal(stream_key, dims, jnp.float32) * width
    if len(pieces) > 0:
        entries = block_scale(stream_key, dims, pieces, -0.22, 0.18) * entries
    return jnp.clip(entries, min=-limit, max=limit).astype(held_as)


def setup_inputs(seed: int = 0) -> dict:
    streams_of = jax.random.split(jax.random.key(seed), 5)
    return {
        "pressure": bell_draw(streams_of[0], (N_LES * FACE_CAP, TIME), 1.0, 6.0, ((0, 8), (1, 4))),
        "targets": draw_targets(jax.random.fold_in(streams_of[4], 71), 0),
        "counts": draw_counts(jax.random.fold_in(streams_of[4], 71), 0),
        "pseudo_inverse": bell_draw(streams_of[3], (STATIONS, MODES, POINTS), POINTS ** -0.5, 0.046875, ((2, 32),)),
    }


def fourier_rows():
    sample_ids = jnp.arange(TIME, dtype=jnp.int32)
    orders = jnp.arange(1, HARM + 1, dtype=jnp.int32)
    phase_ids = orders[:, None] * sample_ids[None, :] % TIME
    angles = phase_ids.astype(jnp.float32) * (2.0 * math.pi / TIME)
    scale_factor = math.sqrt(2.0 / TIME)
    return jnp.stack([jnp.cos(angles), -jnp.sin(angles)]) * scale_factor

def reference(pressure, targets, counts, pseudo_inverse):
    slot_ids = jnp.arange(N_LES * FACE_CAP, dtype=jnp.int32)
    partition = slot_ids // FACE_CAP
    is_live = slot_ids % FACE_CAP < counts[partition]
    rows = jnp.where(is_live, targets, STATIONS * POINTS).astype(jnp.int32)
    station = jnp.zeros((STATIONS * POINTS, TIME), jnp.bfloat16).at[rows].set(pressure, mode='drop')
    fourier = fourier_rows()
    spectra = jnp.einsum('ckt,pt->ckp', fourier, station.astype(jnp.float32), precision=lax.Precision.HIGHEST)
    row_span = POINTS // N_LES
    results = []
    for station_index in range(STATIONS):

        def add_block(block_index, totals, station_index=station_index):
            start = (station_index * POINTS + block_index * row_span).astype(jnp.int32)
            spectra_part = lax.dynamic_slice_in_dim(spectra, start, row_span, 2)
            offset = (block_index * row_span).astype(jnp.int32)
            weights = lax.dynamic_slice_in_dim(pseudo_inverse[station_index], offset, row_span, 1).astype(jnp.float32)
            return totals + jnp.einsum('ckp,mp->ckm', spectra_part, weights, precision=lax.Precision.HIGHEST)
        results.append(lax.fori_loop(0, N_LES, add_block, jnp.zeros((2, HARM, MODES), jnp.float32)))
    return jnp.stack(results)
```

```python
import functools
import math

import jax
import jax.numpy as jnp
from jax import lax
from jax.experimental import pallas as pl
from jax.experimental.pallas import tpu as pltpu
from jax.sharding import PartitionSpec as P

TIME = 512
HARM = 8
COLS = 2 * HARM
LANES = 128
GROUPS = LANES // COLS
UNROLL = 16
VMEM_BYTES = 56 * 1024 * 1024
MESH = pl.DeviceIdType.MESH


def fourier_rows():
    sample_ids = jnp.arange(TIME, dtype=jnp.int32)
    orders = jnp.arange(1, HARM + 1, dtype=jnp.int32)
    phase_ids = orders[:, None] * sample_ids[None, :] % TIME
    angles = phase_ids.astype(jnp.float32) * (2.0 * math.pi / TIME)
    scale_factor = math.sqrt(2.0 / TIME)
    return jnp.stack([jnp.cos(angles), -jnp.sin(angles)]) * scale_factor


def rank_by_owner(dest_les, is_live, les_count):
    face_slots = dest_les.shape[0]
    span_width = math.gcd(face_slots, 128)
    owner_ids = jnp.arange(les_count, dtype=jnp.int32)
    matches = ((dest_les[None, :] == owner_ids[:, None]) & is_live[None, :]).astype(jnp.float32)
    matches = matches.reshape(les_count, face_slots // span_width, span_width)
    position = jnp.arange(span_width, dtype=jnp.int32)
    upper = (position[:, None] <= position[None, :]).astype(jnp.float32)
    within = jnp.einsum("nbj,jw->nbw", matches, upper, precision=lax.Precision.HIGHEST)
    block_sums = jnp.sum(matches, axis=2)
    before = jnp.cumsum(block_sums, axis=1) - block_sums
    running = within + before[:, :, None]
    ranked = jnp.sum(running * matches, axis=0).reshape(face_slots) - 1.0
    totals = jnp.sum(block_sums, axis=1)
    return ranked.astype(jnp.int32), totals.astype(jnp.int32)


def lane_group(shape):
    return lax.broadcasted_iota(jnp.int32, shape, len(shape) - 1) // COLS


def pack_kernel(counts, pos, rows, pressure, basis, out, tags, spectra, placed):
    face_slots = pressure.shape[0]
    chunk = math.gcd(face_slots, 1024)

    @pl.loop(0, face_slots // chunk)
    def _(step):
        at = pl.ds(pl.multiple_of(step * chunk, chunk), chunk)
        block = pressure[at, :]
        spectra[at, :] = jnp.dot(
            block, basis[0], preferred_element_type=jnp.float32
        ) + jnp.dot(block, basis[1], preferred_element_type=jnp.float32)

    @pl.loop(0, (counts[0] + UNROLL - 1) // UNROLL)
    def _(step):
        base = pl.multiple_of(step * UNROLL, UNROLL)
        for at in range(UNROLL):
            where = pos[base + at]
            placed[pl.ds(where, 1), :] = spectra[pl.ds(base + at, 1), :]
            tags[where] = rows[base + at]

    les_count, rank_rows, _ = out.shape
    group = lane_group((rank_rows, LANES))

    @pl.loop(0, les_count)
    def _(owner):
        total = jnp.zeros((rank_rows, LANES), jnp.float32)
        for part in range(GROUPS):
            start = pl.multiple_of((owner * GROUPS + part) * rank_rows, rank_rows)
            total = jnp.where(group == part, placed[pl.ds(start, rank_rows), :], total)
        out[owner] = total


def unpack_kernel(counts, tags, data, out, spread, placed):
    les_count = data.shape[0]
    mode_count, block_rows, _ = out.shape
    rank_rows = spread.shape[0] // (les_count * GROUPS)
    cap = rank_rows * GROUPS

    @pl.loop(0, les_count)
    def _(source):
        block = data[source, pl.ds(0, rank_rows), :]
        for part in range(GROUPS):
            start = pl.multiple_of(source * cap + part * rank_rows, rank_rows)
            moved = block if part == 0 else pltpu.roll(block, LANES - part * COLS, 1)
            spread[pl.ds(start, rank_rows), :] = moved

    @pl.loop(0, les_count)
    def _(source):
        @pl.loop(0, (counts[source] + UNROLL - 1) // UNROLL)
        def _(step):
            base = pl.multiple_of(source * cap + step * UNROLL, UNROLL)
            for at in range(UNROLL):
                placed[pl.ds(tags[base + at], 1), :] = spread[pl.ds(base + at, 1), :]

    group = lane_group((block_rows, LANES))
    halves = GROUPS // 2

    @pl.loop(0, mode_count)
    def _(mode):
        total = jnp.zeros((block_rows, LANES), jnp.float32)
        for part in range(GROUPS):
            station, piece = part // halves, part % halves
            start = (station * mode_count + mode) * halves * block_rows + piece * block_rows
            block = placed[pl.ds(pl.multiple_of(start, block_rows), block_rows), :]
            moved = block if part == 0 else pltpu.roll(block, part * COLS, 1)
            total = jnp.where(group == part, moved, total)
        out[mode] = total


def tail_kernel(
    les_count, mode_count, blocks, pinv, out,
    weights, recv_modes, shares, recv_all,
    load_sem, mode_send, mode_recv, all_send, all_recv,
):
    les, mode = lax.axis_index("les"), lax.axis_index("modes")
    count = les_count * mode_count
    me = les * mode_count + mode
    load = pltpu.make_async_copy(pinv, weights, load_sem)
    load.start()
    barrier = pltpu.get_barrier_semaphore()

    @pl.loop(1, count)
    def _(step):
        peer = lax.rem(me + step, count)
        pl.semaphore_signal(
            barrier, inc=1, device_id=(peer // mode_count, lax.rem(peer, mode_count)),
            device_id_type=MESH,
        )

    pl.semaphore_wait(barrier, count - 1)
    copies = []
    for step in range(1, mode_count):
        peer = lax.rem(mode + step, mode_count)
        copy = pltpu.make_async_remote_copy(
            src_ref=blocks.at[peer],
            dst_ref=recv_modes.at[step - 1],
            send_sem=mode_send.at[step - 1],
            recv_sem=mode_recv.at[step - 1],
            device_id=(les, peer),
            device_id_type=MESH,
        )
        copy.start()
        copies.append(copy)
    total = blocks[mode]
    for step in range(1, mode_count):
        copies[step - 1].wait()
        total = total + recv_modes[step - 1]
    load.wait()
    turned = total.T
    halves = GROUPS // 2
    width = out.shape[2]
    for station in range(2):
        first = station * halves
        rows = jnp.concatenate(
            [turned[(first + at) * COLS:(first + at + 1) * COLS] for at in range(halves)], axis=1
        )
        high = rows.astype(jnp.bfloat16)
        low = (rows - high.astype(jnp.float32)).astype(jnp.bfloat16)
        both = jnp.concatenate([high, low], axis=0)
        projected = lax.dot_general(
            both, weights[station], (((1,), (1,)), ((), ())), preferred_element_type=jnp.float32
        )
        projected = projected[:COLS] + projected[COLS:]
        lane = station * (LANES // 2)
        for peer in range(count):
            shares[peer, :, lane:lane + width] = projected[:, peer * width:(peer + 1) * width]

    @pl.loop(1, count)
    def _(step):
        peer = lax.rem(me + step, count)
        pltpu.make_async_remote_copy(
            src_ref=shares.at[peer],
            dst_ref=recv_all.at[step - 1],
            send_sem=all_send,
            recv_sem=all_recv,
            device_id=(peer // mode_count, lax.rem(peer, mode_count)),
            device_id_type=MESH,
        ).start()

    pltpu.make_async_copy(recv_all, recv_all, all_recv).wait()
    result = shares[me] + jnp.sum(recv_all[...], axis=0)
    for station in range(2):
        lane = station * (LANES // 2)
        out[station] = result[:, lane:lane + width]
    pltpu.make_async_copy(recv_all, recv_all, all_send).wait()


def local(pressure, targets, counts, pseudo_inverse):
    les_count = lax.axis_size("les")
    mode_count = lax.axis_size("modes")
    block_len = pressure.shape[1]
    face_slots = targets.shape[0]
    stations, mode_total, point_dev = pseudo_inverse.shape
    rows_les = point_dev * mode_count
    points_all = rows_les * les_count
    all_rows = stations * rows_les
    send_cap = face_slots // les_count
    send_total = les_count * send_cap
    rank_rows = send_cap // GROUPS
    block_rows = stations * point_dev // GROUPS
    device_count = les_count * mode_count
    vmem = pl.BlockSpec(memory_space=pltpu.VMEM)
    smem = pl.BlockSpec(memory_space=pltpu.SMEM)

    slot_ids = jnp.arange(face_slots, dtype=jnp.int32)
    is_live = slot_ids < counts[0]
    station_of = targets // points_all
    point_of = targets % points_all
    dest_les = point_of // rows_les
    local_row = station_of * rows_les + point_of % rows_les
    face_rank, totals = rank_by_owner(dest_les, is_live, les_count)
    send_pos = jnp.where(is_live, dest_les * send_cap + face_rank, send_total)

    fourier = fourier_rows()
    block_start = lax.axis_index("modes") * block_len
    basis = lax.dynamic_slice_in_dim(fourier, block_start, block_len, 2)
    basis = basis.reshape(COLS, block_len).T
    basis = jnp.tile(basis, (1, GROUPS))
    high = lax.reduce_precision(basis, 8, 7)
    basis = jnp.stack([high, basis - high]).astype(jnp.bfloat16)

    packed, tags = pl.pallas_call(
        pack_kernel,
        out_shape=(
            jax.ShapeDtypeStruct((les_count, rank_rows, LANES), jnp.float32),
            jax.ShapeDtypeStruct((send_total + LANES,), jnp.int32),
        ),
        in_specs=[smem, smem, smem, vmem, vmem],
        out_specs=(vmem, smem),
        scratch_shapes=[
            pltpu.VMEM((face_slots, LANES), jnp.float32),
            pltpu.VMEM((send_total + 8, LANES), jnp.float32),
        ],
        compiler_params=pltpu.CompilerParams(vmem_limit_bytes=VMEM_BYTES),
        name="pack",
    )(counts, send_pos, local_row, pressure, basis)

    rank_ids = jnp.arange(send_cap, dtype=jnp.int32)
    tags = tags[:send_total].reshape(les_count, send_cap)
    tags = jnp.where(rank_ids[None, :] < totals[:, None], tags, all_rows)
    tags = tags.astype(jnp.float32).reshape(les_count, send_cap // LANES, LANES)
    outgoing = jnp.concatenate([packed, tags], axis=1)
    incoming = lax.all_to_all(outgoing, "les", split_axis=0, concat_axis=0, tiled=True)
    tags_in = incoming[:, rank_rows:].astype(jnp.int32).reshape(les_count, send_cap)
    counts_in = jnp.sum((tags_in < all_rows).astype(jnp.int32), axis=1)

    blocks = pl.pallas_call(
        unpack_kernel,
        out_shape=jax.ShapeDtypeStruct((mode_count, block_rows, LANES), jnp.float32),
        in_specs=[smem, smem, vmem],
        out_specs=vmem,
        scratch_shapes=[
            pltpu.VMEM((send_total, LANES), jnp.float32),
            pltpu.VMEM((all_rows + 8, LANES), jnp.float32),
        ],
        compiler_params=pltpu.CompilerParams(vmem_limit_bytes=VMEM_BYTES),
        name="unpack",
    )(counts_in, tags_in.reshape(send_total), incoming)

    width = mode_total // device_count
    result = pl.pallas_call(
        functools.partial(tail_kernel, les_count, mode_count),
        out_shape=jax.ShapeDtypeStruct((stations, COLS, width), jnp.float32),
        in_specs=[vmem, pl.BlockSpec(memory_space=pl.ANY)],
        out_specs=vmem,
        scratch_shapes=[
            pltpu.VMEM((stations, mode_total, point_dev), jnp.bfloat16),
            pltpu.VMEM((mode_count - 1, block_rows, LANES), jnp.float32),
            pltpu.VMEM((device_count, COLS, LANES), jnp.float32),
            pltpu.VMEM((device_count - 1, COLS, LANES), jnp.float32),
            pltpu.SemaphoreType.DMA,
            pltpu.SemaphoreType.DMA((mode_count - 1,)),
            pltpu.SemaphoreType.DMA((mode_count - 1,)),
            pltpu.SemaphoreType.DMA,
            pltpu.SemaphoreType.DMA,
        ],
        compiler_params=pltpu.CompilerParams(
            collective_id=0, has_side_effects=True, vmem_limit_bytes=VMEM_BYTES
        ),
        name="tail",
    )(blocks, pseudo_inverse)
    return result.reshape(stations, 2, HARM, width)


def solution(mesh):
    placed = (P("les", "modes"), P("les"), P("les"), P(None, None, ("les", "modes")))
    return jax.shard_map(
        local,
        mesh=mesh,
        in_specs=placed,
        out_specs=P(None, None, None, ("les", "modes")),
        check_vma=False,
    )
```

```python
import functools
import math

import jax
import jax.numpy as jnp
from jax import lax
from jax.experimental import pallas as pl
from jax.experimental.pallas import tpu as pltpu
from jax.sharding import PartitionSpec as P

TIME = 512
HARM = 8
COLS = 2 * HARM
LANES = 128
GROUPS = LANES // COLS
UNROLL = 16
VMEM_BYTES = 56 * 1024 * 1024
MESH = pl.DeviceIdType.MESH


def fourier_rows():
    sample_ids = jnp.arange(TIME, dtype=jnp.int32)
    orders = jnp.arange(1, HARM + 1, dtype=jnp.int32)
    phase_ids = orders[:, None] * sample_ids[None, :] % TIME
    angles = phase_ids.astype(jnp.float32) * (2.0 * math.pi / TIME)
    scale_factor = math.sqrt(2.0 / TIME)
    return jnp.stack([jnp.cos(angles), -jnp.sin(angles)]) * scale_factor


def lane_group(shape):
    return lax.broadcasted_iota(jnp.int32, shape, len(shape) - 1) // COLS


def pack_kernel(
    rows_les, cap, stride, counts, targets, pressure, basis, out, tags,
    spectra, placed, pos_rows, pos, row_rows, rows, pos_sem, row_sem,
):
    les_count, rank_rows, _ = out.shape
    points_all = rows_les * les_count
    face_slots, block_len = pressure.shape
    lines = targets.shape[0]
    chunk = math.gcd(face_slots, 1024)

    target = targets[...]
    point = target % points_all
    station = target // points_all
    owner_of = point // rows_les
    line = lax.broadcasted_iota(jnp.int32, (lines, LANES), 0)
    lane = lax.broadcasted_iota(jnp.int32, (lines, LANES), 1)
    owner_of = jnp.where(line * LANES + lane < counts[0], owner_of, les_count)
    row_rows[...] = station * rows_les + point % rows_les
    row_copy = pltpu.make_async_copy(row_rows, rows, row_sem)
    row_copy.start()
    first = lax.broadcasted_iota(jnp.int32, (LANES, 2 * LANES), 0)
    second = lax.broadcasted_iota(jnp.int32, (LANES, 2 * LANES), 1)
    upper = ((first <= second) | (second >= LANES)).astype(jnp.bfloat16)
    above = lax.broadcasted_iota(jnp.int32, (lines, lines), 0)
    below = lax.broadcasted_iota(jnp.int32, (lines, lines), 1)
    earlier = (above > below).astype(jnp.bfloat16)
    where = jnp.full((lines, LANES), les_count * stride, jnp.int32)
    for owner in range(les_count):
        chosen = owner_of == owner
        match = jnp.where(chosen, 1.0, 0.0).astype(jnp.bfloat16)
        running = jnp.dot(match, upper, preferred_element_type=jnp.float32)
        within, line_total = running[:, :LANES], running[:, LANES:]
        before = jnp.dot(
            earlier, line_total.astype(jnp.bfloat16), preferred_element_type=jnp.float32
        )
        rank = (within + before).astype(jnp.int32) - 1
        where = jnp.where(chosen, owner * stride + rank, where)
        total = (before + line_total)[lines - 1:lines].astype(jnp.int32)
        pos_rows[lines + owner:lines + owner + 1, :] = total
    pos_rows[:lines, :] = where
    pos_copy = pltpu.make_async_copy(pos_rows, pos, pos_sem)
    pos_copy.start()

    @pl.loop(0, face_slots // chunk)
    def _(step):
        at = pl.ds(pl.multiple_of(step * chunk, chunk), chunk)
        block = pressure[at, :]
        block = jnp.concatenate([block, block], axis=1)
        spectra[at, :] = jnp.dot(block, basis[...], preferred_element_type=jnp.float32)

    row_copy.wait()
    pos_copy.wait()
    steps_line = LANES // UNROLL

    @pl.loop(0, (counts[0] + UNROLL - 1) // UNROLL)
    def _(step):
        base = pl.multiple_of(step * UNROLL, UNROLL)
        line_at = step // steps_line
        lane_at = (step % steps_line) * UNROLL
        for at in range(UNROLL):
            where = pos[line_at, lane_at + at]
            placed[pl.ds(where, 1), :] = spectra[pl.ds(base + at, 1), :]
            tags[where] = rows[line_at, lane_at + at]

    @pl.loop(0, les_count)
    def _(owner):
        tags[owner * stride + cap] = pos[lines + owner, 0]

    group = lane_group((rank_rows, LANES))

    @pl.loop(0, les_count)
    def _(owner):
        total = jnp.zeros((rank_rows, LANES), jnp.float32)
        for part in range(GROUPS):
            start = pl.multiple_of(owner * stride + part * rank_rows, rank_rows)
            total = jnp.where(group == part, placed[pl.ds(start, rank_rows), :], total)
        out[owner] = total


def exchange_kernel(
    les_count, stride, data, tags, data_in, tags_in,
    data_send, data_recv, tags_send, tags_recv, own_sem, own_tags_sem,
):
    les, mode = lax.axis_index("les"), lax.axis_index("modes")
    barrier = pltpu.get_barrier_semaphore()
    for step in range(1, les_count):
        peer = lax.rem(les + step, les_count)
        pl.semaphore_signal(barrier, inc=1, device_id=(peer, mode), device_id_type=MESH)
    own = pltpu.make_async_copy(data.at[les], data_in.at[les], own_sem)
    own_at = pl.ds(pl.multiple_of(les * stride, stride), stride)
    own_tags = pltpu.make_async_copy(tags.at[own_at], tags_in.at[own_at], own_tags_sem)
    own.start()
    own_tags.start()
    pl.semaphore_wait(barrier, les_count - 1)
    copies = []
    for step in range(1, les_count):
        peer = lax.rem(les + step, les_count)
        peer_at = pl.ds(pl.multiple_of(peer * stride, stride), stride)
        copy = pltpu.make_async_remote_copy(
            src_ref=tags.at[peer_at],
            dst_ref=tags_in.at[own_at],
            send_sem=tags_send.at[step - 1],
            recv_sem=tags_recv.at[step - 1],
            device_id=(peer, mode),
            device_id_type=MESH,
        )
        copy.start()
        copies.append(copy)
        copy = pltpu.make_async_remote_copy(
            src_ref=data.at[peer],
            dst_ref=data_in.at[les],
            send_sem=data_send.at[step - 1],
            recv_sem=data_recv.at[step - 1],
            device_id=(peer, mode),
            device_id_type=MESH,
        )
        copy.start()
        copies.append(copy)
    own.wait()
    own_tags.wait()
    for copy in copies:
        copy.wait()


def unpack_kernel(cap, stride, tags, data, out, spread, placed):
    les_count = data.shape[0]
    mode_count, block_rows, _ = out.shape
    rank_rows = spread.shape[0] // (les_count * GROUPS)
    @pl.loop(0, les_count)
    def _(source):
        block = data[source, pl.ds(0, rank_rows), :]
        for part in range(GROUPS):
            start = pl.multiple_of(source * cap + part * rank_rows, rank_rows)
            moved = block if part == 0 else pltpu.roll(block, LANES - part * COLS, 1)
            spread[pl.ds(start, rank_rows), :] = moved

    dump = mode_count * GROUPS * block_rows

    @pl.loop(0, les_count)
    def _(source):
        live = tags[source * stride + cap]

        @pl.loop(0, live // UNROLL)
        def _(step):
            start = pl.multiple_of(step * UNROLL, UNROLL)
            for at in range(UNROLL):
                row = tags[source * stride + start + at]
                placed[pl.ds(row, 1), :] = spread[pl.ds(source * cap + start + at, 1), :]

        @pl.when(live % UNROLL > 0)
        def _():
            start = pl.multiple_of(live // UNROLL * UNROLL, UNROLL)
            base = source * cap + start
            for at in range(UNROLL):
                row = jnp.where(start + at < live, tags[source * stride + start + at], dump)
                placed[pl.ds(row, 1), :] = spread[pl.ds(base + at, 1), :]

    group = lane_group((block_rows, LANES))
    halves = GROUPS // 2

    @pl.loop(0, mode_count)
    def _(mode):
        total = jnp.zeros((block_rows, LANES), jnp.float32)
        for part in range(GROUPS):
            station, piece = part // halves, part % halves
            start = (station * mode_count + mode) * halves * block_rows + piece * block_rows
            block = placed[pl.ds(pl.multiple_of(start, block_rows), block_rows), :]
            moved = block if part == 0 else pltpu.roll(block, part * COLS, 1)
            total = jnp.where(group == part, moved, total)
        out[mode] = total


def tail_kernel(
    les_count, mode_count, blocks, pinv, out,
    weights, recv_modes, shares, recv_les, partial, recv_last, load_sem,
    mode_send, mode_recv, les_send, les_recv, last_send, last_recv,
):
    les, mode = lax.axis_index("les"), lax.axis_index("modes")
    load = pltpu.make_async_copy(pinv, weights, load_sem)
    load.start()
    barrier = pltpu.get_barrier_semaphore()
    for step in range(1, mode_count):
        peer = lax.rem(mode + step, mode_count)
        pl.semaphore_signal(barrier, inc=1, device_id=(les, peer), device_id_type=MESH)
    for step in range(1, les_count):
        peer = lax.rem(les + step, les_count)
        pl.semaphore_signal(barrier, inc=1, device_id=(peer, mode), device_id_type=MESH)
    pl.semaphore_wait(barrier, les_count + mode_count - 2)
    copies = []
    for step in range(1, mode_count):
        peer = lax.rem(mode + step, mode_count)
        copy = pltpu.make_async_remote_copy(
            src_ref=blocks.at[peer],
            dst_ref=recv_modes.at[step - 1],
            send_sem=mode_send.at[step - 1],
            recv_sem=mode_recv.at[step - 1],
            device_id=(les, peer),
            device_id_type=MESH,
        )
        copy.start()
        copies.append(copy)
    total = blocks[mode]
    for step in range(1, mode_count):
        copies[step - 1].wait()
        total = total + recv_modes[step - 1]
    load.wait()
    turned = total.T
    halves = GROUPS // 2
    width = out.shape[2]
    for station in range(2):
        first = station * halves
        rows = jnp.concatenate(
            [turned[(first + at) * COLS:(first + at + 1) * COLS] for at in range(halves)], axis=1
        )
        high = rows.astype(jnp.bfloat16)
        low = (rows - high.astype(jnp.float32)).astype(jnp.bfloat16)
        both = jnp.concatenate([high, low], axis=0)
        projected = lax.dot_general(
            both, weights[station], (((1,), (1,)), ((), ())), preferred_element_type=jnp.float32
        )
        projected = projected[:COLS] + projected[COLS:]
        lane = station * (LANES // 2)
        for peer in range(les_count * mode_count):
            piece = projected[:, peer * width:(peer + 1) * width]
            shares[peer // mode_count, peer % mode_count, :, lane:lane + width] = piece

    copies = []
    for step in range(1, les_count):
        peer = lax.rem(les + step, les_count)
        copy = pltpu.make_async_remote_copy(
            src_ref=shares.at[peer],
            dst_ref=recv_les.at[step - 1],
            send_sem=les_send.at[step - 1],
            recv_sem=les_recv.at[step - 1],
            device_id=(peer, mode),
            device_id_type=MESH,
        )
        copy.start()
        copies.append(copy)
    total = shares[les]
    for step in range(1, les_count):
        copies[step - 1].wait()
        total = total + recv_les[step - 1]
    partial[...] = total
    copies = []
    for step in range(1, mode_count):
        peer = lax.rem(mode + step, mode_count)
        copy = pltpu.make_async_remote_copy(
            src_ref=partial.at[peer],
            dst_ref=recv_last.at[step - 1],
            send_sem=last_send.at[step - 1],
            recv_sem=last_recv.at[step - 1],
            device_id=(les, peer),
            device_id_type=MESH,
        )
        copy.start()
        copies.append(copy)
    result = partial[mode]
    for step in range(1, mode_count):
        copies[step - 1].wait()
        result = result + recv_last[step - 1]
    for station in range(2):
        lane = station * (LANES // 2)
        out[station] = result[:, lane:lane + width]


def local(pressure, targets, counts, pseudo_inverse):
    les_count = lax.axis_size("les")
    mode_count = lax.axis_size("modes")
    block_len = pressure.shape[1]
    face_slots = targets.shape[0]
    stations, mode_total, point_dev = pseudo_inverse.shape
    rows_les = point_dev * mode_count
    all_rows = stations * rows_les
    send_cap = face_slots // les_count
    send_total = les_count * send_cap
    stride = (send_cap // 1024 + 1) * 1024
    lines = face_slots // LANES
    rank_rows = send_cap // GROUPS
    block_rows = stations * point_dev // GROUPS
    device_count = les_count * mode_count
    vmem = pl.BlockSpec(memory_space=pltpu.VMEM)
    smem = pl.BlockSpec(memory_space=pltpu.SMEM)

    fourier = fourier_rows()
    block_start = lax.axis_index("modes") * block_len
    basis = lax.dynamic_slice_in_dim(fourier, block_start, block_len, 2)
    basis = basis.reshape(COLS, block_len).T
    basis = jnp.tile(basis, (1, GROUPS))
    high = lax.reduce_precision(basis, 8, 7)
    basis = jnp.concatenate([high, basis - high]).astype(jnp.bfloat16)

    packed, tags = pl.pallas_call(
        functools.partial(pack_kernel, rows_les, send_cap, stride),
        out_shape=(
            jax.ShapeDtypeStruct((les_count, rank_rows, LANES), jnp.float32),
            jax.ShapeDtypeStruct(((les_count + 1) * stride,), jnp.int32),
        ),
        in_specs=[smem, vmem, vmem, vmem],
        out_specs=(vmem, smem),
        scratch_shapes=[
            pltpu.VMEM((face_slots, LANES), jnp.float32),
            pltpu.VMEM((les_count * stride + 8, LANES), jnp.float32),
            pltpu.VMEM((lines + les_count, LANES), jnp.int32),
            pltpu.SMEM((lines + les_count, LANES), jnp.int32),
            pltpu.VMEM((lines, LANES), jnp.int32),
            pltpu.SMEM((lines, LANES), jnp.int32),
            pltpu.SemaphoreType.DMA,
            pltpu.SemaphoreType.DMA,
        ],
        compiler_params=pltpu.CompilerParams(vmem_limit_bytes=VMEM_BYTES),
        name="pack",
    )(counts, targets.reshape(lines, LANES), pressure, basis)

    hbm = pl.BlockSpec(memory_space=pl.ANY)
    peers = les_count - 1
    data_in, tags_in = pl.pallas_call(
        functools.partial(exchange_kernel, les_count, stride),
        out_shape=(
            jax.ShapeDtypeStruct((les_count, rank_rows, LANES), jnp.float32),
            jax.ShapeDtypeStruct((les_count * stride,), jnp.int32),
        ),
        in_specs=[hbm, hbm],
        out_specs=(hbm, hbm),
        scratch_shapes=[pltpu.SemaphoreType.DMA((peers,))] * 4 + [pltpu.SemaphoreType.DMA] * 2,
        compiler_params=pltpu.CompilerParams(collective_id=1, has_side_effects=True),
        name="exchange",
    )(packed, tags)

    blocks = pl.pallas_call(
        functools.partial(unpack_kernel, send_cap, stride),
        out_shape=jax.ShapeDtypeStruct((mode_count, block_rows, LANES), jnp.float32),
        in_specs=[smem, vmem],
        out_specs=vmem,
        scratch_shapes=[
            pltpu.VMEM((send_total, LANES), jnp.float32),
            pltpu.VMEM((all_rows + 8, LANES), jnp.float32),
        ],
        compiler_params=pltpu.CompilerParams(vmem_limit_bytes=VMEM_BYTES),
        name="unpack",
    )(tags_in, data_in)

    width = mode_total // device_count
    result = pl.pallas_call(
        functools.partial(tail_kernel, les_count, mode_count),
        out_shape=jax.ShapeDtypeStruct((stations, COLS, width), jnp.float32),
        in_specs=[vmem, pl.BlockSpec(memory_space=pl.ANY)],
        out_specs=vmem,
        scratch_shapes=[
            pltpu.VMEM((stations, mode_total, point_dev), jnp.bfloat16),
            pltpu.VMEM((mode_count - 1, block_rows, LANES), jnp.float32),
            pltpu.VMEM((les_count, mode_count, COLS, LANES), jnp.float32),
            pltpu.VMEM((les_count - 1, mode_count, COLS, LANES), jnp.float32),
            pltpu.VMEM((mode_count, COLS, LANES), jnp.float32),
            pltpu.VMEM((mode_count - 1, COLS, LANES), jnp.float32),
            pltpu.SemaphoreType.DMA,
            pltpu.SemaphoreType.DMA((mode_count - 1,)),
            pltpu.SemaphoreType.DMA((mode_count - 1,)),
            pltpu.SemaphoreType.DMA((les_count - 1,)),
            pltpu.SemaphoreType.DMA((les_count - 1,)),
            pltpu.SemaphoreType.DMA((mode_count - 1,)),
            pltpu.SemaphoreType.DMA((mode_count - 1,)),
        ],
        compiler_params=pltpu.CompilerParams(
            collective_id=0, has_side_effects=True, vmem_limit_bytes=VMEM_BYTES
        ),
        name="tail",
    )(blocks, pseudo_inverse)
    return result.reshape(stations, 2, HARM, width)


def solution(mesh):
    placed = (P("les", "modes"), P("les"), P("les"), P(None, None, ("les", "modes")))
    return jax.shard_map(
        local,
        mesh=mesh,
        in_specs=placed,
        out_specs=P(None, None, None, ("les", "modes")),
        check_vma=False,
    )
```

```python
import functools
import math

import jax
import jax.numpy as jnp
import numpy as np
from jax import lax
from jax.experimental import pallas as pl
from jax.experimental.pallas import tpu as pltpu
from jax.sharding import PartitionSpec as P

TIME = 512
HARM = 8
COLS = 2 * HARM
LANES = 128
GROUPS = LANES // COLS
UNROLL = 16
VMEM_BYTES = 56 * 1024 * 1024
MESH = pl.DeviceIdType.MESH


def fourier_columns():
    phase_ids = np.arange(TIME)[:, None] * np.arange(1, HARM + 1)[None, :] % TIME
    angles = phase_ids * (2.0 * math.pi / TIME)
    columns = np.concatenate([np.cos(angles), -np.sin(angles)], axis=1) * math.sqrt(2.0 / TIME)
    columns = np.tile(columns, (1, GROUPS)).astype(np.float32)
    high = columns.astype(jnp.bfloat16)
    low = (columns - high.astype(np.float32)).astype(jnp.bfloat16)
    return np.stack([high, low])


def lane_group(shape):
    return lax.broadcasted_iota(jnp.int32, shape, len(shape) - 1) // COLS


def pack_kernel(
    rows_les, cap, stride, counts, mode_at, targets, pressure, basis, out, tags,
    spectra, placed, pos_rows, pos, row_rows, rows, pos_sem, row_sem,
):
    les_count, rank_rows, _ = out.shape
    points_all = rows_les * les_count
    face_slots, block_len = pressure.shape
    lines = targets.shape[0]
    chunk = math.gcd(face_slots, 1024)

    target = targets[...]
    point = target % points_all
    station = target // points_all
    owner_of = point // rows_les
    line = lax.broadcasted_iota(jnp.int32, (lines, LANES), 0)
    lane = lax.broadcasted_iota(jnp.int32, (lines, LANES), 1)
    owner_of = jnp.where(line * LANES + lane < counts[0], owner_of, les_count)
    row_rows[...] = station * rows_les + point % rows_les
    row_copy = pltpu.make_async_copy(row_rows, rows, row_sem)
    row_copy.start()
    first = lax.broadcasted_iota(jnp.int32, (LANES, 2 * LANES), 0)
    second = lax.broadcasted_iota(jnp.int32, (LANES, 2 * LANES), 1)
    upper = ((first <= second) | (second >= LANES)).astype(jnp.bfloat16)
    above = lax.broadcasted_iota(jnp.int32, (lines, lines), 0)
    below = lax.broadcasted_iota(jnp.int32, (lines, lines), 1)
    earlier = (above > below).astype(jnp.bfloat16)
    where = jnp.full((lines, LANES), les_count * stride, jnp.int32)
    for owner in range(les_count):
        chosen = owner_of == owner
        match = jnp.where(chosen, 1.0, 0.0).astype(jnp.bfloat16)
        running = jnp.dot(match, upper, preferred_element_type=jnp.float32)
        within, line_total = running[:, :LANES], running[:, LANES:]
        before = jnp.dot(
            earlier, line_total.astype(jnp.bfloat16), preferred_element_type=jnp.float32
        )
        rank = (within + before).astype(jnp.int32) - 1
        where = jnp.where(chosen, owner * stride + rank, where)
        total = (before + line_total)[lines - 1:lines].astype(jnp.int32)
        pos_rows[lines + owner:lines + owner + 1, :] = total
    pos_rows[:lines, :] = where
    pos_copy = pltpu.make_async_copy(pos_rows, pos, pos_sem)
    pos_copy.start()

    times = pl.ds(pl.multiple_of(mode_at[0] * block_len, block_len), block_len)
    block_basis = jnp.concatenate([basis[0, times, :], basis[1, times, :]], axis=0)

    @pl.loop(0, face_slots // chunk)
    def _(step):
        at = pl.ds(pl.multiple_of(step * chunk, chunk), chunk)
        block = pressure[at, :]
        block = jnp.concatenate([block, block], axis=1)
        spectra[at, :] = jnp.dot(block, block_basis, preferred_element_type=jnp.float32)

    row_copy.wait()
    pos_copy.wait()

    @pl.loop(0, (counts[0] + LANES - 1) // LANES)
    def _(line_at):
        base = pl.multiple_of(line_at * LANES, LANES)
        for first in range(0, LANES, UNROLL):
            span = range(first, first + UNROLL)
            wheres = [pos[line_at, at] for at in span]
            names = [rows[line_at, at] for at in span]
            values = [spectra[pl.ds(base + at, 1), :] for at in span]
            for where, name, value in zip(wheres, names, values):
                placed[pl.ds(where, 1), :] = value
                tags[where] = name

    @pl.loop(0, les_count)
    def _(owner):
        tags[owner * stride + cap] = pos[lines + owner, 0]

    group = lane_group((rank_rows, LANES))

    @pl.loop(0, les_count)
    def _(owner):
        total = jnp.zeros((rank_rows, LANES), jnp.float32)
        for part in range(GROUPS):
            start = pl.multiple_of(owner * stride + part * rank_rows, rank_rows)
            total = jnp.where(group == part, placed[pl.ds(start, rank_rows), :], total)
        out[owner] = total


def exchange_kernel(
    les_count, stride, data, tags, data_in, tags_in,
    data_send, data_recv, tags_send, tags_recv, own_sem, own_tags_sem,
):
    les, mode = lax.axis_index("les"), lax.axis_index("modes")
    barrier = pltpu.get_barrier_semaphore()
    for step in range(1, les_count):
        peer = lax.rem(les + step, les_count)
        pl.semaphore_signal(barrier, inc=1, device_id=(peer, mode), device_id_type=MESH)
    own = pltpu.make_async_copy(data.at[les], data_in.at[les], own_sem)
    own_at = pl.ds(pl.multiple_of(les * stride, stride), stride)
    own_tags = pltpu.make_async_copy(tags.at[own_at], tags_in.at[own_at], own_tags_sem)
    own.start()
    own_tags.start()
    pl.semaphore_wait(barrier, les_count - 1)
    copies = []
    for step in range(1, les_count):
        peer = lax.rem(les + step, les_count)
        peer_at = pl.ds(pl.multiple_of(peer * stride, stride), stride)
        copy = pltpu.make_async_remote_copy(
            src_ref=tags.at[peer_at],
            dst_ref=tags_in.at[own_at],
            send_sem=tags_send.at[step - 1],
            recv_sem=tags_recv.at[step - 1],
            device_id=(peer, mode),
            device_id_type=MESH,
        )
        copy.start()
        copies.append(copy)
        copy = pltpu.make_async_remote_copy(
            src_ref=data.at[peer],
            dst_ref=data_in.at[les],
            send_sem=data_send.at[step - 1],
            recv_sem=data_recv.at[step - 1],
            device_id=(peer, mode),
            device_id_type=MESH,
        )
        copy.start()
        copies.append(copy)
    own.wait()
    own_tags.wait()
    for copy in copies:
        copy.wait()


def unpack_kernel(cap, stride, tags, data, out, spread, placed):
    les_count = data.shape[0]
    mode_count, block_rows, _ = out.shape
    rank_rows = spread.shape[0] // (les_count * GROUPS)
    @pl.loop(0, les_count)
    def _(source):
        block = data[source, pl.ds(0, rank_rows), :]
        for part in range(GROUPS):
            start = pl.multiple_of(source * cap + part * rank_rows, rank_rows)
            moved = block if part == 0 else pltpu.roll(block, LANES - part * COLS, 1)
            spread[pl.ds(start, rank_rows), :] = moved

    dump = mode_count * GROUPS * block_rows

    @pl.loop(0, les_count)
    def _(source):
        live = tags[source * stride + cap]

        @pl.loop(0, live // UNROLL)
        def _(step):
            start = pl.multiple_of(step * UNROLL, UNROLL)
            base = source * cap + start
            names = [tags[source * stride + start + at] for at in range(UNROLL)]
            values = [spread[pl.ds(base + at, 1), :] for at in range(UNROLL)]
            for name, value in zip(names, values):
                placed[pl.ds(name, 1), :] = value

        @pl.when(live % UNROLL > 0)
        def _():
            start = pl.multiple_of(live // UNROLL * UNROLL, UNROLL)
            base = source * cap + start
            for at in range(UNROLL):
                row = jnp.where(start + at < live, tags[source * stride + start + at], dump)
                placed[pl.ds(row, 1), :] = spread[pl.ds(base + at, 1), :]

    group = lane_group((block_rows, LANES))
    halves = GROUPS // 2

    @pl.loop(0, mode_count)
    def _(mode):
        total = jnp.zeros((block_rows, LANES), jnp.float32)
        for part in range(GROUPS):
            station, piece = part // halves, part % halves
            start = (station * mode_count + mode) * halves * block_rows + piece * block_rows
            block = placed[pl.ds(pl.multiple_of(start, block_rows), block_rows), :]
            moved = block if part == 0 else pltpu.roll(block, part * COLS, 1)
            total = jnp.where(group == part, moved, total)
        out[mode] = total


def share_form(width):
    pieces = 3 if width % 24 == 0 else 1
    return pieces, width // pieces


def tail_kernel(
    les_count, mode_count, blocks, pinv, out,
    weights, whole, recv_modes, shares, recv_les, partial, recv_last, load_sem,
    mode_send, mode_recv, les_send, les_recv, last_send, last_recv,
):
    les, mode = lax.axis_index("les"), lax.axis_index("modes")
    load = pltpu.make_async_copy(pinv, weights, load_sem)
    load.start()
    barrier = pltpu.get_barrier_semaphore()
    for step in range(1, mode_count):
        peer = lax.rem(mode + step, mode_count)
        pl.semaphore_signal(barrier, inc=1, device_id=(les, peer), device_id_type=MESH)
    for step in range(1, les_count):
        peer = lax.rem(les + step, les_count)
        pl.semaphore_signal(barrier, inc=1, device_id=(peer, mode), device_id_type=MESH)
    pl.semaphore_wait(barrier, les_count + mode_count - 2)
    copies = []
    for step in range(1, mode_count):
        peer = lax.rem(mode + step, mode_count)
        copy = pltpu.make_async_remote_copy(
            src_ref=blocks.at[peer],
            dst_ref=recv_modes.at[step - 1],
            send_sem=mode_send.at[step - 1],
            recv_sem=mode_recv.at[step - 1],
            device_id=(les, peer),
            device_id_type=MESH,
        )
        copy.start()
        copies.append(copy)
    total = blocks[mode]
    for step in range(1, mode_count):
        copies[step - 1].wait()
        total = total + recv_modes[step - 1]
    load.wait()
    halves = GROUPS // 2
    width = out.shape[2]
    high = total.astype(jnp.bfloat16).astype(jnp.float32)
    low = total - high
    lane = lax.broadcasted_iota(jnp.int32, total.shape, 1)
    projected = []
    for station in range(2):
        rows = []
        for at in range(halves):
            shift = LANES - (station * halves + at) * COLS
            high_at = pltpu.roll(high, shift % LANES, 1)
            low_at = pltpu.roll(low, (shift + COLS) % LANES, 1)
            both = jnp.where(lane < COLS, high_at, jnp.where(lane < 2 * COLS, low_at, 0.0))
            rows.append(both.astype(jnp.bfloat16))
        result = jnp.dot(
            weights[station], jnp.concatenate(rows, axis=0), preferred_element_type=jnp.float32
        )
        projected.append(result + pltpu.roll(result, LANES - COLS, 1))
    lane = lax.broadcasted_iota(jnp.int32, projected[0].shape, 1)
    second = pltpu.roll(projected[1], COLS, 1)
    both = jnp.where(lane < COLS, projected[0], second)
    whole[...] = jnp.where(lane < 2 * COLS, both, 0.0)
    pieces, piece_rows = share_form(width)
    for peer in range(les_count * mode_count):
        piece = whole[pl.ds(peer * width, piece_rows), :]
        for at in range(1, pieces):
            start = peer * width + at * piece_rows
            piece = piece + pltpu.roll(whole[pl.ds(start, piece_rows), :], at * 2 * COLS, 1)
        shares[peer // mode_count, peer % mode_count, pl.ds(0, piece_rows), :] = piece

    copies = []
    for step in range(1, les_count):
        peer = lax.rem(les + step, les_count)
        copy = pltpu.make_async_remote_copy(
            src_ref=shares.at[peer],
            dst_ref=recv_les.at[step - 1],
            send_sem=les_send.at[step - 1],
            recv_sem=les_recv.at[step - 1],
            device_id=(peer, mode),
            device_id_type=MESH,
        )
        copy.start()
        copies.append(copy)
    total = shares[les]
    for step in range(1, les_count):
        copies[step - 1].wait()
        total = total + recv_les[step - 1]
    partial[...] = total
    copies = []
    for step in range(1, mode_count):
        peer = lax.rem(mode + step, mode_count)
        copy = pltpu.make_async_remote_copy(
            src_ref=partial.at[peer],
            dst_ref=recv_last.at[step - 1],
            send_sem=last_send.at[step - 1],
            recv_sem=last_recv.at[step - 1],
            device_id=(les, peer),
            device_id_type=MESH,
        )
        copy.start()
        copies.append(copy)
    result = partial[mode]
    for step in range(1, mode_count):
        copies[step - 1].wait()
        result = result + recv_last[step - 1]
    turned = result.T
    for station in range(2):
        for at in range(pieces):
            start = (at * 2 + station) * COLS
            piece = turned[start:start + COLS, :piece_rows]
            out[station, :, at * piece_rows:(at + 1) * piece_rows] = piece


def local(pressure, targets, counts, pseudo_inverse):
    les_count = lax.axis_size("les")
    mode_count = lax.axis_size("modes")
    face_slots = targets.shape[0]
    stations, mode_total, point_dev = pseudo_inverse.shape
    rows_les = point_dev * mode_count
    all_rows = stations * rows_les
    send_cap = face_slots // les_count
    send_total = les_count * send_cap
    stride = (send_cap // 1024 + 1) * 1024
    lines = face_slots // LANES
    rank_rows = send_cap // GROUPS
    block_rows = stations * point_dev // GROUPS
    device_count = les_count * mode_count
    vmem = pl.BlockSpec(memory_space=pltpu.VMEM)
    smem = pl.BlockSpec(memory_space=pltpu.SMEM)

    mode_at = lax.axis_index("modes").astype(jnp.int32).reshape(1)

    packed, tags = pl.pallas_call(
        functools.partial(pack_kernel, rows_les, send_cap, stride),
        out_shape=(
            jax.ShapeDtypeStruct((les_count, rank_rows, LANES), jnp.float32),
            jax.ShapeDtypeStruct(((les_count + 1) * stride,), jnp.int32),
        ),
        in_specs=[smem, smem, vmem, vmem, vmem],
        out_specs=(vmem, smem),
        scratch_shapes=[
            pltpu.VMEM((face_slots, LANES), jnp.float32),
            pltpu.VMEM((les_count * stride + 8, LANES), jnp.float32),
            pltpu.VMEM((lines + les_count, LANES), jnp.int32),
            pltpu.SMEM((lines + les_count, LANES), jnp.int32),
            pltpu.VMEM((lines, LANES), jnp.int32),
            pltpu.SMEM((lines, LANES), jnp.int32),
            pltpu.SemaphoreType.DMA,
            pltpu.SemaphoreType.DMA,
        ],
        compiler_params=pltpu.CompilerParams(vmem_limit_bytes=VMEM_BYTES),
        name="pack",
    )(counts, mode_at, targets.reshape(lines, LANES), pressure, jnp.asarray(fourier_columns()))

    hbm = pl.BlockSpec(memory_space=pl.ANY)
    peers = les_count - 1
    data_in, tags_in = pl.pallas_call(
        functools.partial(exchange_kernel, les_count, stride),
        out_shape=(
            jax.ShapeDtypeStruct((les_count, rank_rows, LANES), jnp.float32),
            jax.ShapeDtypeStruct((les_count * stride,), jnp.int32),
        ),
        in_specs=[hbm, hbm],
        out_specs=(hbm, hbm),
        scratch_shapes=[pltpu.SemaphoreType.DMA((peers,))] * 4 + [pltpu.SemaphoreType.DMA] * 2,
        compiler_params=pltpu.CompilerParams(collective_id=1, has_side_effects=True),
        name="exchange",
    )(packed, tags)

    blocks = pl.pallas_call(
        functools.partial(unpack_kernel, send_cap, stride),
        out_shape=jax.ShapeDtypeStruct((mode_count, block_rows, LANES), jnp.float32),
        in_specs=[smem, vmem],
        out_specs=vmem,
        scratch_shapes=[
            pltpu.VMEM((send_total, LANES), jnp.float32),
            pltpu.VMEM((all_rows + 8, LANES), jnp.float32),
        ],
        compiler_params=pltpu.CompilerParams(vmem_limit_bytes=VMEM_BYTES),
        name="unpack",
    )(tags_in, data_in)

    width = mode_total // device_count
    share_rows = (share_form(width)[1] + 7) // 8 * 8
    result = pl.pallas_call(
        functools.partial(tail_kernel, les_count, mode_count),
        out_shape=jax.ShapeDtypeStruct((stations, COLS, width), jnp.float32),
        in_specs=[vmem, pl.BlockSpec(memory_space=pl.ANY)],
        out_specs=vmem,
        scratch_shapes=[
            pltpu.VMEM((stations, mode_total, point_dev), jnp.bfloat16),
            pltpu.VMEM((mode_total, LANES), jnp.float32),
            pltpu.VMEM((mode_count - 1, block_rows, LANES), jnp.float32),
            pltpu.VMEM((les_count, mode_count, share_rows, LANES), jnp.float32),
            pltpu.VMEM((les_count - 1, mode_count, share_rows, LANES), jnp.float32),
            pltpu.VMEM((mode_count, share_rows, LANES), jnp.float32),
            pltpu.VMEM((mode_count - 1, share_rows, LANES), jnp.float32),
            pltpu.SemaphoreType.DMA,
            pltpu.SemaphoreType.DMA((mode_count - 1,)),
            pltpu.SemaphoreType.DMA((mode_count - 1,)),
            pltpu.SemaphoreType.DMA((les_count - 1,)),
            pltpu.SemaphoreType.DMA((les_count - 1,)),
            pltpu.SemaphoreType.DMA((mode_count - 1,)),
            pltpu.SemaphoreType.DMA((mode_count - 1,)),
        ],
        compiler_params=pltpu.CompilerParams(
            collective_id=0, has_side_effects=True, vmem_limit_bytes=VMEM_BYTES
        ),
        name="tail",
    )(blocks, pseudo_inverse)
    return result.reshape(stations, 2, HARM, width)


def solution(mesh):
    placed = (P("les", "modes"), P("les"), P("les"), P(None, None, ("les", "modes")))
    return jax.shard_map(
        local,
        mesh=mesh,
        in_specs=placed,
        out_specs=P(None, None, None, ("les", "modes")),
        check_vma=False,
    )
```

```python
import functools
import math

import jax
import jax.numpy as jnp
import numpy as np
from jax import lax
from jax.experimental import pallas as pl
from jax.experimental.pallas import tpu as pltpu
from jax.sharding import PartitionSpec as P

TIME = 512
HARM = 8
COLS = 2 * HARM
LANES = 128
GROUPS = LANES // COLS
UNROLL = 16
VMEM_BYTES = 56 * 1024 * 1024
MESH = pl.DeviceIdType.MESH


def fourier_columns():
    phase_ids = np.arange(TIME)[:, None] * np.arange(1, HARM + 1)[None, :] % TIME
    angles = phase_ids * (2.0 * math.pi / TIME)
    columns = np.concatenate([np.cos(angles), -np.sin(angles)], axis=1) * math.sqrt(2.0 / TIME)
    columns = np.tile(columns, (1, GROUPS)).astype(np.float32)
    high = columns.astype(jnp.bfloat16)
    low = (columns - high.astype(np.float32)).astype(jnp.bfloat16)
    return np.stack([high, low])


def lane_group(shape):
    return lax.broadcasted_iota(jnp.int32, shape, len(shape) - 1) // COLS


def index_kernel(rows_les, les_count, counts, targets, sources, tags, wheres, names):
    points_all = rows_les * les_count
    lines = targets.shape[0]
    send_lines = sources.shape[0]
    stride = send_lines // les_count * LANES

    target = targets[...]
    point = target % points_all
    station = target // points_all
    owner_of = point // rows_les
    line = lax.broadcasted_iota(jnp.int32, (lines, LANES), 0)
    lane = lax.broadcasted_iota(jnp.int32, (lines, LANES), 1)
    owner_of = jnp.where(line * LANES + lane < counts[0], owner_of, les_count)
    names[...] = station * rows_les + point % rows_les + 1
    first = lax.broadcasted_iota(jnp.int32, (LANES, 2 * LANES), 0)
    second = lax.broadcasted_iota(jnp.int32, (LANES, 2 * LANES), 1)
    upper = ((first <= second) | (second >= LANES)).astype(jnp.bfloat16)
    above = lax.broadcasted_iota(jnp.int32, (lines, lines), 0)
    below = lax.broadcasted_iota(jnp.int32, (lines, lines), 1)
    earlier = (above > below).astype(jnp.bfloat16)
    where = jnp.full((lines, LANES), les_count * stride, jnp.int32)
    for owner in range(les_count):
        chosen = owner_of == owner
        match = jnp.where(chosen, 1.0, 0.0).astype(jnp.bfloat16)
        running = jnp.dot(match, upper, preferred_element_type=jnp.float32)
        within, line_total = running[:, :LANES], running[:, LANES:]
        before = jnp.dot(
            earlier, line_total.astype(jnp.bfloat16), preferred_element_type=jnp.float32
        )
        rank = (within + before).astype(jnp.int32) - 1
        where = jnp.where(chosen, owner * stride + rank, where)
    wheres[...] = where

    line_ids = lax.broadcasted_iota(jnp.int32, (send_lines, LANES), 0)
    lane_ids = lax.broadcasted_iota(jnp.int32, (LANES, LANES), 0)
    face_lane = lax.broadcasted_iota(jnp.int32, (LANES, LANES), 1).astype(jnp.float32)

    def add_lines(step, total):
        lefts, rights = [], []
        for at in range(8):
            line_at = step * 8 + at
            where = wheres[pl.ds(line_at, 1), :]
            name = names[pl.ds(line_at, 1), :]
            left = jnp.where(line_ids == where // LANES, 1.0, 0.0).astype(jnp.bfloat16)
            hit = lane_ids == where % LANES
            face_line = jnp.full((1, LANES), line_at, jnp.int32).astype(jnp.float32)
            parts = [
                jnp.where(hit, face_line, 0.0),
                jnp.where(hit, face_lane, 0.0),
                jnp.where(hit, (name // 64).astype(jnp.float32), 0.0),
                jnp.where(hit, (name % 64).astype(jnp.float32), 0.0),
            ]
            lefts.append(left)
            rights.append(jnp.concatenate(parts, axis=0).astype(jnp.bfloat16))
        return total + lax.dot_general(
            jnp.concatenate(lefts, axis=1),
            jnp.concatenate(rights, axis=1),
            (((1,), (1,)), ((), ())),
            preferred_element_type=jnp.float32,
        )

    total = lax.fori_loop(
        0, lines // 8, add_lines, jnp.zeros((send_lines, 4 * LANES), jnp.float32)
    )
    source = total[:, :LANES] * LANES + total[:, LANES:2 * LANES]
    sources[...] = source.astype(jnp.int32)
    tags[...] = total[:, 2 * LANES:3 * LANES] * 64 + total[:, 3 * LANES:]


def exchange_kernel(
    les_count, mode_count, sources, tags, pressure, basis, data_in,
    spectra, placed, packed, send_sem, recv_sem, own_sem,
):
    les, mode = lax.axis_index("les"), lax.axis_index("modes")
    barrier = pltpu.get_barrier_semaphore()
    for step in range(1, les_count):
        peer = lax.rem(les + step, les_count)
        pl.semaphore_signal(barrier, inc=1, device_id=(peer, mode), device_id_type=MESH)

    face_slots, block_len = pressure.shape
    chunk = math.gcd(face_slots, 1024)
    times = pl.ds(pl.multiple_of(mode * block_len, block_len), block_len)
    block_basis = jnp.concatenate([basis[0, times, :], basis[1, times, :]], axis=0)

    @pl.loop(0, face_slots // chunk)
    def _(step):
        at = pl.ds(pl.multiple_of(step * chunk, chunk), chunk)
        block = pressure[at, :]
        block = jnp.concatenate([block, block], axis=1)
        spectra[at, :] = jnp.dot(block, block_basis, preferred_element_type=jnp.float32)

    cap = placed.shape[0]
    rank_rows = cap // GROUPS
    tag_rows = cap // LANES
    group = lane_group((rank_rows, LANES))

    def fill(owner):
        @pl.loop(0, tag_rows)
        def _(line_at):
            base = pl.multiple_of(line_at * LANES, LANES)
            from_line = owner * tag_rows + line_at
            for first in range(0, LANES, UNROLL):
                span = range(first, first + UNROLL)
                ids = [sources[from_line, at] for at in span]
                values = [spectra[pl.ds(face, 1), :] for face in ids]
                for at, value in zip(span, values):
                    placed[pl.ds(base + at, 1), :] = value

        total = jnp.zeros((rank_rows, LANES), jnp.float32)
        for part in range(GROUPS):
            total = jnp.where(group == part, placed[pl.ds(part * rank_rows, rank_rows), :], total)
        packed[owner, pl.ds(0, rank_rows), :] = total
        packed[owner, pl.ds(rank_rows, tag_rows), :] = tags[owner]

    def remote(step):
        peer = lax.rem(les + step, les_count)
        return peer, pltpu.make_async_remote_copy(
            src_ref=packed.at[peer],
            dst_ref=data_in.at[les],
            send_sem=send_sem.at[step - 1],
            recv_sem=recv_sem.at[step - 1],
            device_id=(peer, mode),
            device_id_type=MESH,
        )

    pl.semaphore_wait(barrier, les_count - 1)

    @pl.loop(1, les_count)
    def _(step):
        peer, copy = remote(step)
        fill(peer)
        copy.start()

    fill(les)
    own = pltpu.make_async_copy(packed.at[les], data_in.at[les], own_sem)
    own.start()
    own.wait()

    @pl.loop(1, les_count)
    def _(step):
        remote(step)[1].wait()


def unpack_kernel(data, out, spread, placed, name_rows, names, name_sem):
    les_count = data.shape[0]
    mode_count, block_rows, _ = out.shape
    rank_rows = spread.shape[0] // (les_count * GROUPS)
    cap = rank_rows * GROUPS
    tag_rows = cap // LANES
    dump = mode_count * GROUPS * block_rows
    lines = les_count * tag_rows

    for source in range(les_count):
        tags = data[source, pl.ds(rank_rows, tag_rows), :]
        live = jnp.where(tags > 0.0, 1.0, 0.0)
        live = jnp.sum(jnp.sum(live, axis=0, keepdims=True), axis=1, keepdims=True)
        live = jnp.broadcast_to(live, (1, LANES)).astype(jnp.int32)
        found = jnp.where(tags > 0.0, tags - 1.0, float(dump)).astype(jnp.int32)
        name_rows[source * tag_rows:(source + 1) * tag_rows, :] = found
        name_rows[lines + source:lines + source + 1, :] = live
    name_copy = pltpu.make_async_copy(name_rows, names, name_sem)
    name_copy.start()

    @pl.loop(0, les_count)
    def _(source):
        block = data[source, pl.ds(0, rank_rows), :]
        for part in range(GROUPS):
            start = pl.multiple_of(source * cap + part * rank_rows, rank_rows)
            moved = block if part == 0 else pltpu.roll(block, LANES - part * COLS, 1)
            spread[pl.ds(start, rank_rows), :] = moved

    name_copy.wait()
    steps_line = LANES // UNROLL

    @pl.loop(0, les_count)
    def _(source):
        @pl.loop(0, (names[lines + source, 0] + UNROLL - 1) // UNROLL)
        def _(step):
            base = pl.multiple_of(source * cap + step * UNROLL, UNROLL)
            line_at = source * tag_rows + step // steps_line
            lane_at = (step % steps_line) * UNROLL
            ids = [names[line_at, lane_at + at] for at in range(UNROLL)]
            values = [spread[pl.ds(base + at, 1), :] for at in range(UNROLL)]
            for name, value in zip(ids, values):
                placed[pl.ds(name, 1), :] = value

    group = lane_group((block_rows, LANES))
    halves = GROUPS // 2

    @pl.loop(0, mode_count)
    def _(mode):
        total = jnp.zeros((block_rows, LANES), jnp.float32)
        for part in range(GROUPS):
            station, piece = part // halves, part % halves
            start = (station * mode_count + mode) * halves * block_rows + piece * block_rows
            block = placed[pl.ds(pl.multiple_of(start, block_rows), block_rows), :]
            moved = block if part == 0 else pltpu.roll(block, part * COLS, 1)
            total = jnp.where(group == part, moved, total)
        out[mode] = total


def share_form(width):
    pieces = 3 if width % 24 == 0 else 1
    return pieces, width // pieces


def tail_kernel(
    les_count, mode_count, blocks, pinv, out,
    weights, whole, recv_modes, shares, recv_les, partial, recv_last, load_sem,
    mode_send, mode_recv, les_send, les_recv, last_send, last_recv,
):
    les, mode = lax.axis_index("les"), lax.axis_index("modes")
    load = pltpu.make_async_copy(pinv, weights, load_sem)
    load.start()
    barrier = pltpu.get_barrier_semaphore()
    for step in range(1, mode_count):
        peer = lax.rem(mode + step, mode_count)
        pl.semaphore_signal(barrier, inc=1, device_id=(les, peer), device_id_type=MESH)
    for step in range(1, les_count):
        peer = lax.rem(les + step, les_count)
        pl.semaphore_signal(barrier, inc=1, device_id=(peer, mode), device_id_type=MESH)
    pl.semaphore_wait(barrier, les_count + mode_count - 2)
    copies = []
    for step in range(1, mode_count):
        peer = lax.rem(mode + step, mode_count)
        copy = pltpu.make_async_remote_copy(
            src_ref=blocks.at[peer],
            dst_ref=recv_modes.at[step - 1],
            send_sem=mode_send.at[step - 1],
            recv_sem=mode_recv.at[step - 1],
            device_id=(les, peer),
            device_id_type=MESH,
        )
        copy.start()
        copies.append(copy)
    total = blocks[mode]
    for step in range(1, mode_count):
        copies[step - 1].wait()
        total = total + recv_modes[step - 1]
    load.wait()
    halves = GROUPS // 2
    width = out.shape[2]
    high = total.astype(jnp.bfloat16).astype(jnp.float32)
    low = total - high
    lane = lax.broadcasted_iota(jnp.int32, total.shape, 1)
    projected = []
    for station in range(2):
        rows = []
        for at in range(halves):
            shift = LANES - (station * halves + at) * COLS
            high_at = pltpu.roll(high, shift % LANES, 1)
            low_at = pltpu.roll(low, (shift + COLS) % LANES, 1)
            both = jnp.where(lane < COLS, high_at, jnp.where(lane < 2 * COLS, low_at, 0.0))
            rows.append(both.astype(jnp.bfloat16))
        result = jnp.dot(
            weights[station], jnp.concatenate(rows, axis=0), preferred_element_type=jnp.float32
        )
        projected.append(result + pltpu.roll(result, LANES - COLS, 1))
    lane = lax.broadcasted_iota(jnp.int32, projected[0].shape, 1)
    second = pltpu.roll(projected[1], COLS, 1)
    both = jnp.where(lane < COLS, projected[0], second)
    whole[...] = jnp.where(lane < 2 * COLS, both, 0.0)
    pieces, piece_rows = share_form(width)
    for peer in range(les_count * mode_count):
        piece = whole[pl.ds(peer * width, piece_rows), :]
        for at in range(1, pieces):
            start = peer * width + at * piece_rows
            piece = piece + pltpu.roll(whole[pl.ds(start, piece_rows), :], at * 2 * COLS, 1)
        shares[peer // mode_count, peer % mode_count, pl.ds(0, piece_rows), :] = piece

    copies = []
    for step in range(1, les_count):
        peer = lax.rem(les + step, les_count)
        copy = pltpu.make_async_remote_copy(
            src_ref=shares.at[peer],
            dst_ref=recv_les.at[step - 1],
            send_sem=les_send.at[step - 1],
            recv_sem=les_recv.at[step - 1],
            device_id=(peer, mode),
            device_id_type=MESH,
        )
        copy.start()
        copies.append(copy)
    total = shares[les]
    for step in range(1, les_count):
        copies[step - 1].wait()
        total = total + recv_les[step - 1]
    partial[...] = total
    copies = []
    for step in range(1, mode_count):
        peer = lax.rem(mode + step, mode_count)
        copy = pltpu.make_async_remote_copy(
            src_ref=partial.at[peer],
            dst_ref=recv_last.at[step - 1],
            send_sem=last_send.at[step - 1],
            recv_sem=last_recv.at[step - 1],
            device_id=(les, peer),
            device_id_type=MESH,
        )
        copy.start()
        copies.append(copy)
    result = partial[mode]
    for step in range(1, mode_count):
        copies[step - 1].wait()
        result = result + recv_last[step - 1]
    turned = result.T
    for station in range(2):
        for at in range(pieces):
            start = (at * 2 + station) * COLS
            piece = turned[start:start + COLS, :piece_rows]
            out[station, :, at * piece_rows:(at + 1) * piece_rows] = piece


def local(pressure, targets, counts, pseudo_inverse):
    les_count = lax.axis_size("les")
    mode_count = lax.axis_size("modes")
    face_slots = targets.shape[0]
    stations, mode_total, point_dev = pseudo_inverse.shape
    rows_les = point_dev * mode_count
    all_rows = stations * rows_les
    send_cap = face_slots // les_count
    send_total = les_count * send_cap
    lines = face_slots // LANES
    rank_rows = send_cap // GROUPS
    block_rows = stations * point_dev // GROUPS
    device_count = les_count * mode_count
    vmem = pl.BlockSpec(memory_space=pltpu.VMEM)
    smem = pl.BlockSpec(memory_space=pltpu.SMEM)

    tag_rows = send_cap // LANES
    sources, tags = pl.pallas_call(
        functools.partial(index_kernel, rows_les, les_count),
        out_shape=(
            jax.ShapeDtypeStruct((send_total // LANES, LANES), jnp.int32),
            jax.ShapeDtypeStruct((send_total // LANES, LANES), jnp.float32),
        ),
        in_specs=[smem, vmem],
        out_specs=(vmem, vmem),
        scratch_shapes=[pltpu.VMEM((lines, LANES), jnp.int32)] * 2,
        compiler_params=pltpu.CompilerParams(vmem_limit_bytes=VMEM_BYTES),
        name="index",
    )(counts, targets.reshape(lines, LANES))

    peers = les_count - 1
    data_in = pl.pallas_call(
        functools.partial(exchange_kernel, les_count, mode_count),
        out_shape=jax.ShapeDtypeStruct((les_count, rank_rows + tag_rows, LANES), jnp.float32),
        in_specs=[smem, vmem, vmem, vmem],
        out_specs=vmem,
        scratch_shapes=[
            pltpu.VMEM((face_slots, LANES), jnp.float32),
            pltpu.VMEM((send_cap, LANES), jnp.float32),
            pltpu.VMEM((les_count, rank_rows + tag_rows, LANES), jnp.float32),
            pltpu.SemaphoreType.DMA((peers,)),
            pltpu.SemaphoreType.DMA((peers,)),
            pltpu.SemaphoreType.DMA,
        ],
        compiler_params=pltpu.CompilerParams(
            collective_id=1, has_side_effects=True, vmem_limit_bytes=VMEM_BYTES
        ),
        name="exchange",
    )(
        sources, tags.reshape(les_count, tag_rows, LANES), pressure,
        jnp.asarray(fourier_columns()),
    )

    blocks = pl.pallas_call(
        unpack_kernel,
        out_shape=jax.ShapeDtypeStruct((mode_count, block_rows, LANES), jnp.float32),
        in_specs=[vmem],
        out_specs=vmem,
        scratch_shapes=[
            pltpu.VMEM((send_total, LANES), jnp.float32),
            pltpu.VMEM((all_rows + 8, LANES), jnp.float32),
            pltpu.VMEM((send_total // LANES + les_count, LANES), jnp.int32),
            pltpu.SMEM((send_total // LANES + les_count, LANES), jnp.int32),
            pltpu.SemaphoreType.DMA,
        ],
        compiler_params=pltpu.CompilerParams(vmem_limit_bytes=VMEM_BYTES),
        name="unpack",
    )(data_in)

    width = mode_total // device_count
    share_rows = (share_form(width)[1] + 7) // 8 * 8
    result = pl.pallas_call(
        functools.partial(tail_kernel, les_count, mode_count),
        out_shape=jax.ShapeDtypeStruct((stations, COLS, width), jnp.float32),
        in_specs=[vmem, pl.BlockSpec(memory_space=pl.ANY)],
        out_specs=vmem,
        scratch_shapes=[
            pltpu.VMEM((stations, mode_total, point_dev), jnp.bfloat16),
            pltpu.VMEM((mode_total, LANES), jnp.float32),
            pltpu.VMEM((mode_count - 1, block_rows, LANES), jnp.float32),
            pltpu.VMEM((les_count, mode_count, share_rows, LANES), jnp.float32),
            pltpu.VMEM((les_count - 1, mode_count, share_rows, LANES), jnp.float32),
            pltpu.VMEM((mode_count, share_rows, LANES), jnp.float32),
            pltpu.VMEM((mode_count - 1, share_rows, LANES), jnp.float32),
            pltpu.SemaphoreType.DMA,
            pltpu.SemaphoreType.DMA((mode_count - 1,)),
            pltpu.SemaphoreType.DMA((mode_count - 1,)),
            pltpu.SemaphoreType.DMA((les_count - 1,)),
            pltpu.SemaphoreType.DMA((les_count - 1,)),
            pltpu.SemaphoreType.DMA((mode_count - 1,)),
            pltpu.SemaphoreType.DMA((mode_count - 1,)),
        ],
        compiler_params=pltpu.CompilerParams(
            collective_id=0, has_side_effects=True, vmem_limit_bytes=VMEM_BYTES
        ),
        name="tail",
    )(blocks, pseudo_inverse)
    return result.reshape(stations, 2, HARM, width)


def solution(mesh):
    placed = (P("les", "modes"), P("les"), P("les"), P(None, None, ("les", "modes")))
    return jax.shard_map(
        local,
        mesh=mesh,
        in_specs=placed,
        out_specs=P(None, None, None, ("les", "modes")),
        check_vma=False,
    )
```

```python
import functools
import math

import jax
import jax.numpy as jnp
import numpy as np
from jax import lax
from jax.experimental import pallas as pl
from jax.experimental.pallas import tpu as pltpu
from jax.sharding import PartitionSpec as P

TIME = 512
HARM = 8
COLS = 2 * HARM
LANES = 128
GROUPS = LANES // COLS
UNROLL = 16
VMEM_BYTES = 56 * 1024 * 1024
MESH = pl.DeviceIdType.MESH


def fourier_columns():
    phase_ids = np.arange(TIME)[:, None] * np.arange(1, HARM + 1)[None, :] % TIME
    angles = phase_ids * (2.0 * math.pi / TIME)
    columns = np.concatenate([np.cos(angles), -np.sin(angles)], axis=1) * math.sqrt(2.0 / TIME)
    columns = np.tile(columns, (1, GROUPS)).astype(np.float32)
    high = columns.astype(jnp.bfloat16)
    low = (columns - high.astype(np.float32)).astype(jnp.bfloat16)
    return np.stack([high, low])


def lane_group(shape):
    return lax.broadcasted_iota(jnp.int32, shape, len(shape) - 1) // COLS


def index_kernel(rows_les, les_count, counts, targets, sources, tags, wheres, names):
    points_all = rows_les * les_count
    lines = targets.shape[0]
    send_lines = sources.shape[0]
    stride = send_lines // les_count * LANES

    target = targets[...]
    point = target % points_all
    station = target // points_all
    owner_of = point // rows_les
    line = lax.broadcasted_iota(jnp.int32, (lines, LANES), 0)
    lane = lax.broadcasted_iota(jnp.int32, (lines, LANES), 1)
    owner_of = jnp.where(line * LANES + lane < counts[0], owner_of, les_count)
    names[...] = station * rows_les + point % rows_les + 1
    first = lax.broadcasted_iota(jnp.int32, (LANES, 2 * LANES), 0)
    second = lax.broadcasted_iota(jnp.int32, (LANES, 2 * LANES), 1)
    upper = ((first <= second) | (second >= LANES)).astype(jnp.bfloat16)
    above = lax.broadcasted_iota(jnp.int32, (lines, lines), 0)
    below = lax.broadcasted_iota(jnp.int32, (lines, lines), 1)
    earlier = (above > below).astype(jnp.bfloat16)
    where = jnp.full((lines, LANES), les_count * stride, jnp.int32)
    for owner in range(les_count):
        chosen = owner_of == owner
        match = jnp.where(chosen, 1.0, 0.0).astype(jnp.bfloat16)
        running = jnp.dot(match, upper, preferred_element_type=jnp.float32)
        within, line_total = running[:, :LANES], running[:, LANES:]
        before = jnp.dot(
            earlier, line_total.astype(jnp.bfloat16), preferred_element_type=jnp.float32
        )
        rank = (within + before).astype(jnp.int32) - 1
        where = jnp.where(chosen, owner * stride + rank, where)
    wheres[...] = where

    line_ids = lax.broadcasted_iota(jnp.int32, (send_lines, LANES), 0)
    lane_ids = lax.broadcasted_iota(jnp.int32, (LANES, LANES), 0)
    face_lane = lax.broadcasted_iota(jnp.int32, (LANES, LANES), 1).astype(jnp.float32)

    def add_lines(step, total):
        lefts, rights = [], []
        for at in range(8):
            line_at = step * 8 + at
            where = wheres[pl.ds(line_at, 1), :]
            name = names[pl.ds(line_at, 1), :]
            left = jnp.where(line_ids == where // LANES, 1.0, 0.0).astype(jnp.bfloat16)
            hit = lane_ids == where % LANES
            face_line = jnp.full((1, LANES), line_at, jnp.int32).astype(jnp.float32)
            parts = [
                jnp.where(hit, face_line, 0.0),
                jnp.where(hit, face_lane, 0.0),
                jnp.where(hit, (name // 64).astype(jnp.float32), 0.0),
                jnp.where(hit, (name % 64).astype(jnp.float32), 0.0),
            ]
            lefts.append(left)
            rights.append(jnp.concatenate(parts, axis=0).astype(jnp.bfloat16))
        return total + lax.dot_general(
            jnp.concatenate(lefts, axis=1),
            jnp.concatenate(rights, axis=1),
            (((1,), (1,)), ((), ())),
            preferred_element_type=jnp.float32,
        )

    total = lax.fori_loop(
        0, lines // 8, add_lines, jnp.zeros((send_lines, 4 * LANES), jnp.float32)
    )
    source = total[:, :LANES] * LANES + total[:, LANES:2 * LANES]
    sources[...] = source.astype(jnp.int32)
    tags[...] = total[:, 2 * LANES:3 * LANES] * 64 + total[:, 3 * LANES:]


def exchange_kernel(
    les_count, mode_count, sources, tags, pressure, basis, data_in,
    samples, spectra, placed, packed, load_sem, send_sem, recv_sem, own_sem,
):
    les, mode = lax.axis_index("les"), lax.axis_index("modes")
    face_slots, block_len = pressure.shape
    chunk = math.gcd(face_slots, 1024)

    def load(step):
        at = pl.ds(pl.multiple_of(step * chunk, chunk), chunk)
        return pltpu.make_async_copy(pressure.at[at], samples.at[at], load_sem.at[step])

    for step in range(face_slots // chunk):
        load(step).start()
    barrier = pltpu.get_barrier_semaphore()
    for step in range(1, les_count):
        peer = lax.rem(les + step, les_count)
        pl.semaphore_signal(barrier, inc=1, device_id=(peer, mode), device_id_type=MESH)

    times = pl.ds(pl.multiple_of(mode * block_len, block_len), block_len)
    block_basis = jnp.concatenate([basis[0, times, :], basis[1, times, :]], axis=0)

    @pl.loop(0, face_slots // chunk)
    def _(step):
        at = pl.ds(pl.multiple_of(step * chunk, chunk), chunk)
        load(step).wait()
        block = samples[at, :]
        block = jnp.concatenate([block, block], axis=1)
        spectra[at, :] = jnp.dot(block, block_basis, preferred_element_type=jnp.float32)

    cap = placed.shape[0]
    rank_rows = cap // GROUPS
    tag_rows = cap // LANES
    group = lane_group((rank_rows, LANES))

    def fill(owner):
        @pl.loop(0, tag_rows)
        def _(line_at):
            base = pl.multiple_of(line_at * LANES, LANES)
            from_line = owner * tag_rows + line_at
            for first in range(0, LANES, UNROLL):
                span = range(first, first + UNROLL)
                ids = [sources[from_line, at] for at in span]
                values = [spectra[pl.ds(face, 1), :] for face in ids]
                for at, value in zip(span, values):
                    placed[pl.ds(base + at, 1), :] = value

        total = jnp.zeros((rank_rows, LANES), jnp.float32)
        for part in range(GROUPS):
            total = jnp.where(group == part, placed[pl.ds(part * rank_rows, rank_rows), :], total)
        packed[owner, pl.ds(0, rank_rows), :] = total
        packed[owner, pl.ds(rank_rows, tag_rows), :] = tags[owner]

    def remote(step):
        peer = lax.rem(les + step, les_count)
        return peer, pltpu.make_async_remote_copy(
            src_ref=packed.at[peer],
            dst_ref=data_in.at[les],
            send_sem=send_sem.at[step - 1],
            recv_sem=recv_sem.at[step - 1],
            device_id=(peer, mode),
            device_id_type=MESH,
        )

    pl.semaphore_wait(barrier, les_count - 1)

    @pl.loop(1, les_count)
    def _(step):
        peer, copy = remote(step)
        fill(peer)
        copy.start()

    fill(les)
    own = pltpu.make_async_copy(packed.at[les], data_in.at[les], own_sem)
    own.start()
    own.wait()

    @pl.loop(1, les_count)
    def _(step):
        remote(step)[1].wait()


def unpack_kernel(data, out, spread, placed, name_rows, names, name_sem):
    les_count = data.shape[0]
    mode_count, block_rows, _ = out.shape
    rank_rows = spread.shape[0] // (les_count * GROUPS)
    cap = rank_rows * GROUPS
    tag_rows = cap // LANES
    dump = mode_count * GROUPS * block_rows
    lines = les_count * tag_rows

    for source in range(les_count):
        tags = data[source, pl.ds(rank_rows, tag_rows), :]
        live = jnp.where(tags > 0.0, 1.0, 0.0)
        live = jnp.sum(jnp.sum(live, axis=0, keepdims=True), axis=1, keepdims=True)
        live = jnp.broadcast_to(live, (1, LANES)).astype(jnp.int32)
        found = jnp.where(tags > 0.0, tags - 1.0, float(dump)).astype(jnp.int32)
        name_rows[source * tag_rows:(source + 1) * tag_rows, :] = found
        name_rows[lines + source:lines + source + 1, :] = live
    name_copy = pltpu.make_async_copy(name_rows, names, name_sem)
    name_copy.start()

    @pl.loop(0, les_count)
    def _(source):
        block = data[source, pl.ds(0, rank_rows), :]
        for part in range(GROUPS):
            start = pl.multiple_of(source * cap + part * rank_rows, rank_rows)
            moved = block if part == 0 else pltpu.roll(block, LANES - part * COLS, 1)
            spread[pl.ds(start, rank_rows), :] = moved

    name_copy.wait()

    @pl.loop(0, les_count)
    def _(source):
        live = names[lines + source, 0]

        @pl.loop(0, (live + LANES - 1) // LANES)
        def _(part):
            line_at = source * tag_rows + part
            base = pl.multiple_of(line_at * LANES, LANES)
            for first in range(0, LANES, 2 * UNROLL):

                @pl.when(part * LANES + first < live)
                def _(first=first):
                    for begin in range(first, first + 2 * UNROLL, UNROLL):
                        span = range(begin, begin + UNROLL)
                        ids = [names[line_at, at] for at in span]
                        values = [spread[pl.ds(base + at, 1), :] for at in span]
                        for name, value in zip(ids, values):
                            placed[pl.ds(name, 1), :] = value

    group = lane_group((block_rows, LANES))
    halves = GROUPS // 2

    @pl.loop(0, mode_count)
    def _(mode):
        total = jnp.zeros((block_rows, LANES), jnp.float32)
        for part in range(GROUPS):
            station, piece = part // halves, part % halves
            start = (station * mode_count + mode) * halves * block_rows + piece * block_rows
            block = placed[pl.ds(pl.multiple_of(start, block_rows), block_rows), :]
            moved = block if part == 0 else pltpu.roll(block, part * COLS, 1)
            total = jnp.where(group == part, moved, total)
        out[mode] = total


def share_form(width):
    pieces = 3 if width % 24 == 0 else 1
    return pieces, width // pieces


def tail_kernel(
    les_count, mode_count, blocks, pinv, out,
    weights, whole, recv_modes, shares, recv_les, partial, recv_last, load_sem,
    mode_send, mode_recv, les_send, les_recv, last_send, last_recv,
):
    les, mode = lax.axis_index("les"), lax.axis_index("modes")
    load = pltpu.make_async_copy(pinv, weights, load_sem)
    load.start()
    barrier = pltpu.get_barrier_semaphore()
    for step in range(1, mode_count):
        peer = lax.rem(mode + step, mode_count)
        pl.semaphore_signal(barrier, inc=1, device_id=(les, peer), device_id_type=MESH)
    for step in range(1, les_count):
        peer = lax.rem(les + step, les_count)
        pl.semaphore_signal(barrier, inc=1, device_id=(peer, mode), device_id_type=MESH)
    pl.semaphore_wait(barrier, les_count + mode_count - 2)
    copies = []
    for step in range(1, mode_count):
        peer = lax.rem(mode + step, mode_count)
        copy = pltpu.make_async_remote_copy(
            src_ref=blocks.at[peer],
            dst_ref=recv_modes.at[step - 1],
            send_sem=mode_send.at[step - 1],
            recv_sem=mode_recv.at[step - 1],
            device_id=(les, peer),
            device_id_type=MESH,
        )
        copy.start()
        copies.append(copy)
    total = blocks[mode]
    for step in range(1, mode_count):
        copies[step - 1].wait()
        total = total + recv_modes[step - 1]
    load.wait()
    halves = GROUPS // 2
    width = out.shape[2]
    high = total.astype(jnp.bfloat16).astype(jnp.float32)
    low = total - high
    lane = lax.broadcasted_iota(jnp.int32, total.shape, 1)
    projected = []
    for station in range(2):
        rows = []
        for at in range(halves):
            shift = LANES - (station * halves + at) * COLS
            high_at = pltpu.roll(high, shift % LANES, 1)
            low_at = pltpu.roll(low, (shift + COLS) % LANES, 1)
            both = jnp.where(lane < COLS, high_at, jnp.where(lane < 2 * COLS, low_at, 0.0))
            rows.append(both.astype(jnp.bfloat16))
        result = jnp.dot(
            weights[station], jnp.concatenate(rows, axis=0), preferred_element_type=jnp.float32
        )
        projected.append(result + pltpu.roll(result, LANES - COLS, 1))
    lane = lax.broadcasted_iota(jnp.int32, projected[0].shape, 1)
    second = pltpu.roll(projected[1], COLS, 1)
    both = jnp.where(lane < COLS, projected[0], second)
    whole[...] = jnp.where(lane < 2 * COLS, both, 0.0)
    pieces, piece_rows = share_form(width)
    for peer in range(les_count * mode_count):
        piece = whole[pl.ds(peer * width, piece_rows), :]
        for at in range(1, pieces):
            start = peer * width + at * piece_rows
            piece = piece + pltpu.roll(whole[pl.ds(start, piece_rows), :], at * 2 * COLS, 1)
        shares[peer // mode_count, peer % mode_count, pl.ds(0, piece_rows), :] = piece

    copies = []
    for step in range(1, les_count):
        peer = lax.rem(les + step, les_count)
        copy = pltpu.make_async_remote_copy(
            src_ref=shares.at[peer],
            dst_ref=recv_les.at[step - 1],
            send_sem=les_send.at[step - 1],
            recv_sem=les_recv.at[step - 1],
            device_id=(peer, mode),
            device_id_type=MESH,
        )
        copy.start()
        copies.append(copy)
    total = shares[les]
    for step in range(1, les_count):
        copies[step - 1].wait()
        total = total + recv_les[step - 1]
    partial[...] = total
    copies = []
    for step in range(1, mode_count):
        peer = lax.rem(mode + step, mode_count)
        copy = pltpu.make_async_remote_copy(
            src_ref=partial.at[peer],
            dst_ref=recv_last.at[step - 1],
            send_sem=last_send.at[step - 1],
            recv_sem=last_recv.at[step - 1],
            device_id=(les, peer),
            device_id_type=MESH,
        )
        copy.start()
        copies.append(copy)
    result = partial[mode]
    for step in range(1, mode_count):
        copies[step - 1].wait()
        result = result + recv_last[step - 1]
    turned = result.T
    for station in range(2):
        for at in range(pieces):
            start = (at * 2 + station) * COLS
            piece = turned[start:start + COLS, :piece_rows]
            out[station, :, at * piece_rows:(at + 1) * piece_rows] = piece


def local(pressure, targets, counts, pseudo_inverse):
    les_count = lax.axis_size("les")
    mode_count = lax.axis_size("modes")
    face_slots = targets.shape[0]
    stations, mode_total, point_dev = pseudo_inverse.shape
    rows_les = point_dev * mode_count
    all_rows = stations * rows_les
    send_cap = face_slots // les_count
    send_total = les_count * send_cap
    lines = face_slots // LANES
    rank_rows = send_cap // GROUPS
    block_rows = stations * point_dev // GROUPS
    device_count = les_count * mode_count
    vmem = pl.BlockSpec(memory_space=pltpu.VMEM)
    smem = pl.BlockSpec(memory_space=pltpu.SMEM)

    tag_rows = send_cap // LANES
    sources, tags = pl.pallas_call(
        functools.partial(index_kernel, rows_les, les_count),
        out_shape=(
            jax.ShapeDtypeStruct((send_total // LANES, LANES), jnp.int32),
            jax.ShapeDtypeStruct((send_total // LANES, LANES), jnp.float32),
        ),
        in_specs=[smem, vmem],
        out_specs=(vmem, vmem),
        scratch_shapes=[pltpu.VMEM((lines, LANES), jnp.int32)] * 2,
        compiler_params=pltpu.CompilerParams(vmem_limit_bytes=VMEM_BYTES),
        name="index",
    )(counts, targets.reshape(lines, LANES))

    peers = les_count - 1
    data_in = pl.pallas_call(
        functools.partial(exchange_kernel, les_count, mode_count),
        out_shape=jax.ShapeDtypeStruct((les_count, rank_rows + tag_rows, LANES), jnp.float32),
        in_specs=[smem, vmem, pl.BlockSpec(memory_space=pl.ANY), vmem],
        out_specs=vmem,
        scratch_shapes=[
            pltpu.VMEM(pressure.shape, pressure.dtype),
            pltpu.VMEM((face_slots, LANES), jnp.float32),
            pltpu.VMEM((send_cap, LANES), jnp.float32),
            pltpu.VMEM((les_count, rank_rows + tag_rows, LANES), jnp.float32),
            pltpu.SemaphoreType.DMA((face_slots // math.gcd(face_slots, 1024),)),
            pltpu.SemaphoreType.DMA((peers,)),
            pltpu.SemaphoreType.DMA((peers,)),
            pltpu.SemaphoreType.DMA,
        ],
        compiler_params=pltpu.CompilerParams(
            collective_id=1, has_side_effects=True, vmem_limit_bytes=VMEM_BYTES
        ),
        name="exchange",
    )(
        sources, tags.reshape(les_count, tag_rows, LANES), pressure,
        jnp.asarray(fourier_columns()),
    )

    blocks = pl.pallas_call(
        unpack_kernel,
        out_shape=jax.ShapeDtypeStruct((mode_count, block_rows, LANES), jnp.float32),
        in_specs=[vmem],
        out_specs=vmem,
        scratch_shapes=[
            pltpu.VMEM((send_total, LANES), jnp.float32),
            pltpu.VMEM((all_rows + 8, LANES), jnp.float32),
            pltpu.VMEM((send_total // LANES + les_count, LANES), jnp.int32),
            pltpu.SMEM((send_total // LANES + les_count, LANES), jnp.int32),
            pltpu.SemaphoreType.DMA,
        ],
        compiler_params=pltpu.CompilerParams(vmem_limit_bytes=VMEM_BYTES),
        name="unpack",
    )(data_in)

    width = mode_total // device_count
    share_rows = (share_form(width)[1] + 7) // 8 * 8
    result = pl.pallas_call(
        functools.partial(tail_kernel, les_count, mode_count),
        out_shape=jax.ShapeDtypeStruct((stations, COLS, width), jnp.float32),
        in_specs=[vmem, pl.BlockSpec(memory_space=pl.ANY)],
        out_specs=vmem,
        scratch_shapes=[
            pltpu.VMEM((stations, mode_total, point_dev), jnp.bfloat16),
            pltpu.VMEM((mode_total, LANES), jnp.float32),
            pltpu.VMEM((mode_count - 1, block_rows, LANES), jnp.float32),
            pltpu.VMEM((les_count, mode_count, share_rows, LANES), jnp.float32),
            pltpu.VMEM((les_count - 1, mode_count, share_rows, LANES), jnp.float32),
            pltpu.VMEM((mode_count, share_rows, LANES), jnp.float32),
            pltpu.VMEM((mode_count - 1, share_rows, LANES), jnp.float32),
            pltpu.SemaphoreType.DMA,
            pltpu.SemaphoreType.DMA((mode_count - 1,)),
            pltpu.SemaphoreType.DMA((mode_count - 1,)),
            pltpu.SemaphoreType.DMA((les_count - 1,)),
            pltpu.SemaphoreType.DMA((les_count - 1,)),
            pltpu.SemaphoreType.DMA((mode_count - 1,)),
            pltpu.SemaphoreType.DMA((mode_count - 1,)),
        ],
        compiler_params=pltpu.CompilerParams(
            collective_id=0, has_side_effects=True, vmem_limit_bytes=VMEM_BYTES
        ),
        name="tail",
    )(blocks, pseudo_inverse)
    return result.reshape(stations, 2, HARM, width)


def solution(mesh):
    placed = (P("les", "modes"), P("les"), P("les"), P(None, None, ("les", "modes")))
    return jax.shard_map(
        local,
        mesh=mesh,
        in_specs=placed,
        out_specs=P(None, None, None, ("les", "modes")),
        check_vma=False,
    )
```

```python
import functools
import math

import jax
import jax.numpy as jnp
import numpy as np
from jax import lax
from jax.experimental import pallas as pl
from jax.experimental.pallas import tpu as pltpu
from jax.sharding import PartitionSpec as P

TIME = 512
HARM = 8
COLS = 2 * HARM
LANES = 128
GROUPS = LANES // COLS
UNROLL = 16
VMEM_BYTES = 56 * 1024 * 1024
MESH = pl.DeviceIdType.MESH


def fourier_columns():
    phase_ids = np.arange(TIME)[:, None] * np.arange(1, HARM + 1)[None, :] % TIME
    angles = phase_ids * (2.0 * math.pi / TIME)
    columns = np.concatenate([np.cos(angles), -np.sin(angles)], axis=1) * math.sqrt(2.0 / TIME)
    columns = np.tile(columns, (1, GROUPS)).astype(np.float32)
    high = columns.astype(jnp.bfloat16)
    low = (columns - high.astype(np.float32)).astype(jnp.bfloat16)
    return np.stack([high, low])


def lane_group(shape):
    return lax.broadcasted_iota(jnp.int32, shape, len(shape) - 1) // COLS


def index_kernel(rows_les, les_count, counts, targets, sources, tags, wheres, names):
    points_all = rows_les * les_count
    lines = targets.shape[0]
    send_lines = sources.shape[0]
    stride = send_lines // les_count * LANES

    target = targets[...]
    point = target % points_all
    station = target // points_all
    owner_of = point // rows_les
    line = lax.broadcasted_iota(jnp.int32, (lines, LANES), 0)
    lane = lax.broadcasted_iota(jnp.int32, (lines, LANES), 1)
    owner_of = jnp.where(line * LANES + lane < counts[0], owner_of, les_count)
    names[...] = station * rows_les + point % rows_les + 1
    first = lax.broadcasted_iota(jnp.int32, (LANES, 2 * LANES), 0)
    second = lax.broadcasted_iota(jnp.int32, (LANES, 2 * LANES), 1)
    upper = ((first <= second) | (second >= LANES)).astype(jnp.bfloat16)
    above = lax.broadcasted_iota(jnp.int32, (lines, lines), 0)
    below = lax.broadcasted_iota(jnp.int32, (lines, lines), 1)
    earlier = (above > below).astype(jnp.bfloat16)
    where = jnp.full((lines, LANES), les_count * stride, jnp.int32)
    for owner in range(les_count):
        chosen = owner_of == owner
        match = jnp.where(chosen, 1.0, 0.0).astype(jnp.bfloat16)
        running = jnp.dot(match, upper, preferred_element_type=jnp.float32)
        within, line_total = running[:, :LANES], running[:, LANES:]
        before = jnp.dot(
            earlier, line_total.astype(jnp.bfloat16), preferred_element_type=jnp.float32
        )
        rank = (within + before).astype(jnp.int32) - 1
        where = jnp.where(chosen, owner * stride + rank, where)
    wheres[...] = where

    line_ids = lax.broadcasted_iota(jnp.int32, (send_lines, LANES), 0)
    lane_ids = lax.broadcasted_iota(jnp.int32, (LANES, LANES), 0)
    face_lane = lax.broadcasted_iota(jnp.int32, (LANES, LANES), 1).astype(jnp.float32)

    def add_lines(step, total):
        lefts, rights = [], []
        for at in range(8):
            line_at = step * 8 + at
            where = wheres[pl.ds(line_at, 1), :]
            name = names[pl.ds(line_at, 1), :]
            left = jnp.where(line_ids == where // LANES, 1.0, 0.0).astype(jnp.bfloat16)
            hit = lane_ids == where % LANES
            face_line = jnp.full((1, LANES), line_at, jnp.int32).astype(jnp.float32)
            parts = [
                jnp.where(hit, face_line, 0.0),
                jnp.where(hit, face_lane, 0.0),
                jnp.where(hit, (name // 64).astype(jnp.float32), 0.0),
                jnp.where(hit, (name % 64).astype(jnp.float32), 0.0),
            ]
            lefts.append(left)
            rights.append(jnp.concatenate(parts, axis=0).astype(jnp.bfloat16))
        return total + lax.dot_general(
            jnp.concatenate(lefts, axis=1),
            jnp.concatenate(rights, axis=1),
            (((1,), (1,)), ((), ())),
            preferred_element_type=jnp.float32,
        )

    total = lax.fori_loop(
        0, lines // 8, add_lines, jnp.zeros((send_lines, 4 * LANES), jnp.float32)
    )
    source = total[:, :LANES] * LANES + total[:, LANES:2 * LANES]
    sources[...] = source.astype(jnp.int32)
    tags[...] = total[:, 2 * LANES:3 * LANES] * 64 + total[:, 3 * LANES:]


def exchange_kernel(
    les_count, mode_count, sources, tags, pressure, basis, data_in,
    spectra, placed, packed, send_sem, recv_sem, own_sem,
):
    les, mode = lax.axis_index("les"), lax.axis_index("modes")
    face_slots, block_len = pressure.shape
    chunk = math.gcd(face_slots, 1024)

    barrier = pltpu.get_barrier_semaphore()
    for step in range(1, les_count):
        peer = lax.rem(les + step, les_count)
        pl.semaphore_signal(barrier, inc=1, device_id=(peer, mode), device_id_type=MESH)

    times = pl.ds(pl.multiple_of(mode * block_len, block_len), block_len)
    block_basis = jnp.concatenate([basis[0, times, :], basis[1, times, :]], axis=0)

    @pl.loop(0, face_slots // chunk)
    def _(step):
        at = pl.ds(pl.multiple_of(step * chunk, chunk), chunk)
        block = pressure[at, :]
        block = jnp.concatenate([block, block], axis=1)
        spectra[at, :] = jnp.dot(block, block_basis, preferred_element_type=jnp.float32)

    cap = placed.shape[0]
    rank_rows = cap // GROUPS
    tag_rows = cap // LANES
    group = lane_group((rank_rows, LANES))

    def fill(owner):
        @pl.loop(0, tag_rows)
        def _(line_at):
            base = pl.multiple_of(line_at * LANES, LANES)
            from_line = owner * tag_rows + line_at
            for first in range(0, LANES, UNROLL):
                span = range(first, first + UNROLL)
                ids = [sources[from_line, at] for at in span]
                values = [spectra[pl.ds(face, 1), :] for face in ids]
                for at, value in zip(span, values):
                    placed[pl.ds(base + at, 1), :] = value

        total = jnp.zeros((rank_rows, LANES), jnp.float32)
        for part in range(GROUPS):
            total = jnp.where(group == part, placed[pl.ds(part * rank_rows, rank_rows), :], total)
        packed[owner, pl.ds(0, rank_rows), :] = total
        packed[owner, pl.ds(rank_rows, tag_rows), :] = tags[owner]

    def remote(step):
        peer = lax.rem(les + step, les_count)
        return peer, pltpu.make_async_remote_copy(
            src_ref=packed.at[peer],
            dst_ref=data_in.at[les],
            send_sem=send_sem.at[step - 1],
            recv_sem=recv_sem.at[step - 1],
            device_id=(peer, mode),
            device_id_type=MESH,
        )

    pl.semaphore_wait(barrier, les_count - 1)

    @pl.loop(1, les_count)
    def _(step):
        peer, copy = remote(step)
        fill(peer)
        copy.start()

    fill(les)
    own = pltpu.make_async_copy(packed.at[les], data_in.at[les], own_sem)
    own.start()
    own.wait()

    @pl.loop(1, les_count)
    def _(step):
        remote(step)[1].wait()


def unpack_kernel(data, out, spread, placed, name_rows, names, name_sem):
    les_count = data.shape[0]
    mode_count, block_rows, _ = out.shape
    rank_rows = spread.shape[0] // (les_count * GROUPS)
    cap = rank_rows * GROUPS
    tag_rows = cap // LANES
    dump = mode_count * GROUPS * block_rows
    lines = les_count * tag_rows

    for source in range(les_count):
        tags = data[source, pl.ds(rank_rows, tag_rows), :]
        live = jnp.where(tags > 0.0, 1.0, 0.0)
        live = jnp.sum(jnp.sum(live, axis=0, keepdims=True), axis=1, keepdims=True)
        live = jnp.broadcast_to(live, (1, LANES)).astype(jnp.int32)
        found = jnp.where(tags > 0.0, tags - 1.0, float(dump)).astype(jnp.int32)
        name_rows[source * tag_rows:(source + 1) * tag_rows, :] = found
        name_rows[lines + source:lines + source + 1, :] = live
    name_copy = pltpu.make_async_copy(name_rows, names, name_sem)
    name_copy.start()

    @pl.loop(0, les_count)
    def _(source):
        block = data[source, pl.ds(0, rank_rows), :]
        for part in range(GROUPS):
            start = pl.multiple_of(source * cap + part * rank_rows, rank_rows)
            moved = block if part == 0 else pltpu.roll(block, LANES - part * COLS, 1)
            spread[pl.ds(start, rank_rows), :] = moved

    name_copy.wait()

    @pl.loop(0, les_count)
    def _(source):
        live = names[lines + source, 0]

        @pl.loop(0, (live + LANES - 1) // LANES)
        def _(part):
            line_at = source * tag_rows + part
            base = pl.multiple_of(line_at * LANES, LANES)
            for first in range(0, LANES, 2 * UNROLL):

                @pl.when(part * LANES + first < live)
                def _(first=first):
                    for begin in range(first, first + 2 * UNROLL, UNROLL):
                        span = range(begin, begin + UNROLL)
                        ids = [names[line_at, at] for at in span]
                        values = [spread[pl.ds(base + at, 1), :] for at in span]
                        for name, value in zip(ids, values):
                            placed[pl.ds(name, 1), :] = value

    group = lane_group((block_rows, LANES))
    halves = GROUPS // 2

    @pl.loop(0, mode_count)
    def _(mode):
        total = jnp.zeros((block_rows, LANES), jnp.float32)
        for part in range(GROUPS):
            station, piece = part // halves, part % halves
            start = (station * mode_count + mode) * halves * block_rows + piece * block_rows
            block = placed[pl.ds(pl.multiple_of(start, block_rows), block_rows), :]
            moved = block if part == 0 else pltpu.roll(block, part * COLS, 1)
            total = jnp.where(group == part, moved, total)
        out[mode] = total


def share_form(width):
    pieces = 3 if width % 24 == 0 else 1
    return pieces, width // pieces


def tail_kernel(
    les_count, mode_count, blocks, pinv, out,
    weights, whole, recv_modes, shares, recv_les, partial, recv_last, load_sem,
    mode_send, mode_recv, les_send, les_recv, last_send, last_recv,
):
    les, mode = lax.axis_index("les"), lax.axis_index("modes")
    load = pltpu.make_async_copy(pinv, weights, load_sem)
    load.start()
    barrier = pltpu.get_barrier_semaphore()
    for step in range(1, mode_count):
        peer = lax.rem(mode + step, mode_count)
        pl.semaphore_signal(barrier, inc=1, device_id=(les, peer), device_id_type=MESH)
    for step in range(1, les_count):
        peer = lax.rem(les + step, les_count)
        pl.semaphore_signal(barrier, inc=1, device_id=(peer, mode), device_id_type=MESH)
    pl.semaphore_wait(barrier, les_count + mode_count - 2)
    copies = []
    for step in range(1, mode_count):
        peer = lax.rem(mode + step, mode_count)
        copy = pltpu.make_async_remote_copy(
            src_ref=blocks.at[peer],
            dst_ref=recv_modes.at[step - 1],
            send_sem=mode_send.at[step - 1],
            recv_sem=mode_recv.at[step - 1],
            device_id=(les, peer),
            device_id_type=MESH,
        )
        copy.start()
        copies.append(copy)
    total = blocks[mode]
    for step in range(1, mode_count):
        copies[step - 1].wait()
        total = total + recv_modes[step - 1]
    load.wait()
    halves = GROUPS // 2
    width = out.shape[2]
    high = total.astype(jnp.bfloat16).astype(jnp.float32)
    low = total - high
    lane = lax.broadcasted_iota(jnp.int32, total.shape, 1)
    projected = []
    for station in range(2):
        rows = []
        for at in range(halves):
            shift = LANES - (station * halves + at) * COLS
            high_at = pltpu.roll(high, shift % LANES, 1)
            low_at = pltpu.roll(low, (shift + COLS) % LANES, 1)
            both = jnp.where(lane < COLS, high_at, jnp.where(lane < 2 * COLS, low_at, 0.0))
            rows.append(both.astype(jnp.bfloat16))
        result = jnp.dot(
            weights[station], jnp.concatenate(rows, axis=0), preferred_element_type=jnp.float32
        )
        projected.append(result + pltpu.roll(result, LANES - COLS, 1))
    lane = lax.broadcasted_iota(jnp.int32, projected[0].shape, 1)
    second = pltpu.roll(projected[1], COLS, 1)
    both = jnp.where(lane < COLS, projected[0], second)
    whole[...] = jnp.where(lane < 2 * COLS, both, 0.0)
    pieces, piece_rows = share_form(width)
    for peer in range(les_count * mode_count):
        piece = whole[pl.ds(peer * width, piece_rows), :]
        for at in range(1, pieces):
            start = peer * width + at * piece_rows
            piece = piece + pltpu.roll(whole[pl.ds(start, piece_rows), :], at * 2 * COLS, 1)
        shares[peer // mode_count, peer % mode_count, pl.ds(0, piece_rows), :] = piece

    copies = []
    for step in range(1, les_count):
        peer = lax.rem(les + step, les_count)
        copy = pltpu.make_async_remote_copy(
            src_ref=shares.at[peer],
            dst_ref=recv_les.at[step - 1],
            send_sem=les_send.at[step - 1],
            recv_sem=les_recv.at[step - 1],
            device_id=(peer, mode),
            device_id_type=MESH,
        )
        copy.start()
        copies.append(copy)
    total = shares[les]
    for step in range(1, les_count):
        copies[step - 1].wait()
        total = total + recv_les[step - 1]
    partial[...] = total
    copies = []
    for step in range(1, mode_count):
        peer = lax.rem(mode + step, mode_count)
        copy = pltpu.make_async_remote_copy(
            src_ref=partial.at[peer],
            dst_ref=recv_last.at[step - 1],
            send_sem=last_send.at[step - 1],
            recv_sem=last_recv.at[step - 1],
            device_id=(les, peer),
            device_id_type=MESH,
        )
        copy.start()
        copies.append(copy)
    result = partial[mode]
    for step in range(1, mode_count):
        copies[step - 1].wait()
        result = result + recv_last[step - 1]
    turned = result.T
    for station in range(2):
        for at in range(pieces):
            start = (at * 2 + station) * COLS
            piece = turned[start:start + COLS, :piece_rows]
            out[station, :, at * piece_rows:(at + 1) * piece_rows] = piece


def local(pressure, targets, counts, pseudo_inverse):
    les_count = lax.axis_size("les")
    mode_count = lax.axis_size("modes")
    face_slots = targets.shape[0]
    stations, mode_total, point_dev = pseudo_inverse.shape
    rows_les = point_dev * mode_count
    all_rows = stations * rows_les
    send_cap = face_slots // les_count
    send_total = les_count * send_cap
    lines = face_slots // LANES
    rank_rows = send_cap // GROUPS
    block_rows = stations * point_dev // GROUPS
    device_count = les_count * mode_count
    vmem = pl.BlockSpec(memory_space=pltpu.VMEM)
    smem = pl.BlockSpec(memory_space=pltpu.SMEM)

    tag_rows = send_cap // LANES
    sources, tags = pl.pallas_call(
        functools.partial(index_kernel, rows_les, les_count),
        out_shape=(
            jax.ShapeDtypeStruct((send_total // LANES, LANES), jnp.int32),
            jax.ShapeDtypeStruct((send_total // LANES, LANES), jnp.float32),
        ),
        in_specs=[smem, vmem],
        out_specs=(vmem, vmem),
        scratch_shapes=[pltpu.VMEM((lines, LANES), jnp.int32)] * 2,
        compiler_params=pltpu.CompilerParams(vmem_limit_bytes=VMEM_BYTES),
        name="index",
    )(counts, targets.reshape(lines, LANES))

    peers = les_count - 1
    data_in = pl.pallas_call(
        functools.partial(exchange_kernel, les_count, mode_count),
        out_shape=jax.ShapeDtypeStruct((les_count, rank_rows + tag_rows, LANES), jnp.float32),
        in_specs=[smem, vmem, vmem, vmem],
        out_specs=vmem,
        scratch_shapes=[
            pltpu.VMEM((face_slots, LANES), jnp.float32),
            pltpu.VMEM((send_cap, LANES), jnp.float32),
            pltpu.VMEM((les_count, rank_rows + tag_rows, LANES), jnp.float32),
            pltpu.SemaphoreType.DMA((peers,)),
            pltpu.SemaphoreType.DMA((peers,)),
            pltpu.SemaphoreType.DMA,
        ],
        compiler_params=pltpu.CompilerParams(
            collective_id=1, has_side_effects=True, vmem_limit_bytes=VMEM_BYTES
        ),
        name="exchange",
    )(
        sources, tags.reshape(les_count, tag_rows, LANES), pressure,
        jnp.asarray(fourier_columns()),
    )

    blocks = pl.pallas_call(
        unpack_kernel,
        out_shape=jax.ShapeDtypeStruct((mode_count, block_rows, LANES), jnp.float32),
        in_specs=[vmem],
        out_specs=vmem,
        scratch_shapes=[
            pltpu.VMEM((send_total, LANES), jnp.float32),
            pltpu.VMEM((all_rows + 8, LANES), jnp.float32),
            pltpu.VMEM((send_total // LANES + les_count, LANES), jnp.int32),
            pltpu.SMEM((send_total // LANES + les_count, LANES), jnp.int32),
            pltpu.SemaphoreType.DMA,
        ],
        compiler_params=pltpu.CompilerParams(vmem_limit_bytes=VMEM_BYTES),
        name="unpack",
    )(data_in)

    width = mode_total // device_count
    share_rows = (share_form(width)[1] + 7) // 8 * 8
    result = pl.pallas_call(
        functools.partial(tail_kernel, les_count, mode_count),
        out_shape=jax.ShapeDtypeStruct((stations, COLS, width), jnp.float32),
        in_specs=[vmem, pl.BlockSpec(memory_space=pl.ANY)],
        out_specs=vmem,
        scratch_shapes=[
            pltpu.VMEM((stations, mode_total, point_dev), jnp.bfloat16),
            pltpu.VMEM((mode_total, LANES), jnp.float32),
            pltpu.VMEM((mode_count - 1, block_rows, LANES), jnp.float32),
            pltpu.VMEM((les_count, mode_count, share_rows, LANES), jnp.float32),
            pltpu.VMEM((les_count - 1, mode_count, share_rows, LANES), jnp.float32),
            pltpu.VMEM((mode_count, share_rows, LANES), jnp.float32),
            pltpu.VMEM((mode_count - 1, share_rows, LANES), jnp.float32),
            pltpu.SemaphoreType.DMA,
            pltpu.SemaphoreType.DMA((mode_count - 1,)),
            pltpu.SemaphoreType.DMA((mode_count - 1,)),
            pltpu.SemaphoreType.DMA((les_count - 1,)),
            pltpu.SemaphoreType.DMA((les_count - 1,)),
            pltpu.SemaphoreType.DMA((mode_count - 1,)),
            pltpu.SemaphoreType.DMA((mode_count - 1,)),
        ],
        compiler_params=pltpu.CompilerParams(
            collective_id=0, has_side_effects=True, vmem_limit_bytes=VMEM_BYTES
        ),
        name="tail",
    )(blocks, pseudo_inverse)
    return result.reshape(stations, 2, HARM, width)


def solution(mesh):
    placed = (P("les", "modes"), P("les"), P("les"), P(None, None, ("les", "modes")))
    return jax.shard_map(
        local,
        mesh=mesh,
        in_specs=placed,
        out_specs=P(None, None, None, ("les", "modes")),
        check_vma=False,
    )
```
